32 devices in a mesh: ens: 2 (over y), gx: 4 (over z), gy: 4 (over x, core).
Axes of the slice: x: 2, y: 2, z: 4, core: 2. Of those that a mesh axis runs over, the one named last changes fastest.
Arguments:
- log_cond: float32 [64, 512, 128], P(('ens', 'gx'), 'gy'), parts along dimension 0, may hold values from -1 to 1
- checkpoint: float32 [64, 512, 128], P(('ens', 'gx'), 'gy'), parts along dimension 0, may hold values from 0 to 1
- survey: float32 [64, 512, 128], P(('ens', 'gx'), 'gy'), parts along dimension 0, may hold values from 0 to 1
- survey_weight: float32 [64, 512, 128], P(('ens', 'gx'), 'gy'), parts along dimension 0, may hold values from 0.5 to 5
- well_cells: int32 [512], P('ens'), parts along dimension 0, may hold values from 0 to 2097151
- well_data: float32 [512], P('ens'), parts along dimension 0, may hold values from 0 to 1
- well_weight: float32 [512], P('ens'), parts along dimension 0, may hold values from 1 to 10
- source_cells: int32 [128], P('ens'), parts along dimension 0, may hold values from 0 to 2097151
- source_rate: float32 [128], P('ens'), parts along dimension 0, may hold values from 5 to 20
- step_number: int32 [2], P('ens'), parts along dimension 0, may hold values from 0 to 1999
Outputs:
- log_cond_grad: float32 [64, 512, 128], P(('ens', 'gx'), 'gy'), parts along dimension 0
- checkpoint_adjoint: float32 [64, 512, 128], P(('ens', 'gx'), 'gy'), parts along dimension 0
- concentration: float32 [64, 512, 128], P(('ens', 'gx'), 'gy'), parts along dimension 0
- misfit: float32 [2], P('ens'), parts along dimension 0
The draws below stay inside these ranges and needn't reach their ends.
There are 2 independent parts, one for each index of `ens`. The reference program is written for one: setup_inputs(seed, part) draws one part's arguments, and reference() takes and returns one part's arrays. A program takes and returns all parts, laid end to end along the dimension named above; each array names one. Nothing has to cross between parts.
Inputs may be any that keep to these rules, and one draw needn't show every extreme that they name: `well_cells`: flat cell index (x * 512 + y) * 128 + z. `source_cells`: flat cell index (x * 512 + y) * 128 + z.
All inputs are finite; a program needn't handle non-finite values.
Results may differ from the reference program's by a relative error of at most 0.00002.
Values sent between devices are 32-bit elements; how exact they have to be, the bound alone decides.
A program may use at most 64 MiB of HBM per device.

```python
import math
import jax
import jax.numpy as jnp

NOBS = 256
NSRC = 64
NX = 32
NY = 512
NZ = 128


def place_ends(result, own_key, low, largest):
    longest = result.shape.index(max(result.shape))
    spots = []
    for shift in (0, 1):
        where = [jax.random.randint(jax.random.fold_in(own_key, axis), (), 0, length) for axis, length in enumerate(result.shape)]
        where[longest] = (where[longest] + shift) % result.shape[longest]
        spots.append(tuple(where))
    return result.at[spots[0]].set(low).at[spots[1]].set(largest)


def block_scale(key, extent, cuts, low, top_value):
    def one(position, parts):
        heights = jax.random.uniform(jax.random.fold_in(jax.random.fold_in(key, 6), position), (parts,), jnp.float32, low / len(cuts), top_value / len(cuts))
        return jnp.repeat(jnp.exp(heights), extent[position] // parts).reshape((-1,) + (1,) * (len(extent) - position - 1))

    level = one(*cuts[0])
    for cut in cuts[1:]:
        level = level * one(*cut)
    return level


def setup_inputs(seed: int = 0, part: int = 0) -> dict:
    seeds = jax.random.split(jax.random.key(seed), 11)
    own_keys = jax.random.split(jax.random.fold_in(seeds[10], part), 11)
    return {
        "log_cond": jnp.clip(jax.random.uniform(own_keys[0], (NX, NY, NZ), jnp.float32, -1.0, 1.0) * block_scale(own_keys[0], (NX, NY, NZ), ((0, 4), (1, 4)), -0.4, 0.0), -1.0, 1.0),
        "checkpoint": jnp.clip(1.0 * jax.random.uniform(own_keys[1], (NX, NY, NZ), jnp.float32) ** block_scale(own_keys[1], (NX, NY, NZ), ((0, 4), (1, 4)), -0.2, 0.2), 0.0, 1.0),
        "survey": jnp.clip(1.0 * jax.random.uniform(own_keys[2], (NX, NY, NZ), jnp.float32) ** block_scale(own_keys[2], (NX, NY, NZ), ((0, 4), (1, 4)), -0.2, 0.2), 0.0, 1.0),
        "survey_weight": jnp.clip(jnp.exp(math.log(5.0) - 2.3025851 * jax.random.uniform(own_keys[3], (NX, NY, NZ), jnp.float32) ** block_scale(own_keys[3], (NX, NY, NZ), ((0, 4), (1, 4)), -0.2, 0.2)), 0.5, 5.0),
        "well_cells": place_ends(jax.random.randint(own_keys[4], (NOBS,), 0, NX * NY * NZ), jax.random.fold_in(own_keys[4], 1), 0, (NX * NY * NZ) - 1).astype(jnp.int32),
        "well_data": jnp.clip(jax.random.uniform(own_keys[5], (NOBS,), jnp.float32, 0.0, 1.0), 0.0, 1.0),
        "well_weight": jnp.clip(jnp.exp(jax.random.uniform(own_keys[6], (NOBS,), jnp.float32, math.log(1.0), math.log(10.0))), 1.0, 10.0),
        "source_cells": place_ends(jax.random.randint(own_keys[7], (NSRC,), 0, NX * NY * NZ), jax.random.fold_in(own_keys[7], 1), 0, (NX * NY * NZ) - 1).astype(jnp.int32),
        "source_rate": jnp.clip(jax.random.uniform(own_keys[8], (NSRC,), jnp.float32, 5.0, 20.0), 5.0, 20.0),
        "step_number": jax.random.randint(own_keys[9], (1,), 0, 2000).astype(jnp.int32),
    }


time_step = 0.2
head_slope = 0.5
molecular = 0.05
dispersivity = 0.1

def step_forward(tracer, log_cond, source):
    cond_x = jnp.exp(0.5 * (log_cond[:-1] + log_cond[1:]))
    cond_y = jnp.exp(0.5 * (log_cond[:, :-1] + log_cond[:, 1:]))
    cond_z = jnp.exp(0.5 * (log_cond[:, :, :-1] + log_cond[:, :, 1:]))
    flux_x = head_slope * cond_x * tracer[:-1] - (molecular + dispersivity * cond_x) * (tracer[1:] - tracer[:-1])
    flux_y = -(molecular + dispersivity * cond_y) * (tracer[:, 1:] - tracer[:, :-1])
    flux_z = -(molecular + dispersivity * cond_z) * (tracer[:, :, 1:] - tracer[:, :, :-1])
    pad_x = jnp.pad(flux_x, ((1, 1), (0, 0), (0, 0)))
    pad_y = jnp.pad(flux_y, ((0, 0), (1, 1), (0, 0)))
    pad_z = jnp.pad(flux_z, ((0, 0), (0, 0), (1, 1)))
    spread = pad_x[1:] - pad_x[:-1] + (pad_y[:, 1:] - pad_y[:, :-1]) + (pad_z[:, :, 1:] - pad_z[:, :, :-1])
    return tracer - time_step * spread + time_step * source

def place(cells, values):
    blank = jnp.zeros((NX * NY * NZ,), jnp.float32)
    return blank.at[cells].add(values).reshape(NX, NY, NZ)

def reference(log_cond, checkpoint, survey, survey_weight, well_cells, well_data, well_weight, source_cells, source_rate, step_number):
    clock = step_number.astype(jnp.float32)[0]
    source_first = place(source_cells, source_rate * (1.0 + 0.5 * jnp.sin(0.05 * clock)))
    source_second = place(source_cells, source_rate * (1.0 + 0.5 * jnp.sin(0.05 * (clock + 1.0))))

    def objective(cond_field, start_field):
        middle = step_forward(start_field, cond_field, source_first)
        final = step_forward(middle, cond_field, source_second)
        missed = final - survey
        nearby = final.reshape(-1)[well_cells] - well_data
        value = 0.5 * jnp.sum(survey_weight * missed * missed) + 0.5 * jnp.sum(well_weight * nearby * nearby)
        return (value, final)
    value, pullback, final = jax.vjp(objective, log_cond, checkpoint, has_aux=True)
    grad_cond, grad_start = pullback(jnp.ones_like(value))
    misfit = (value / (NX * NY * NZ)).reshape(1)
    return (grad_cond, grad_start, final, misfit)
```

```python
import functools

import jax
import jax.numpy as jnp
from jax import lax
from jax.experimental import pallas as pl
from jax.experimental.pallas import tpu as pltpu
from jax.sharding import PartitionSpec as P

time_step = 0.2
head_slope = 0.5
molecular = 0.05
dispersivity = 0.1

RIM = 2
PAD = 8
DIRS = ((1, 0), (-1, 0), (0, 1), (0, -1), (1, 1), (1, -1), (-1, 1), (-1, -1))
MESH = pl.DeviceIdType.MESH


def split3(values):
    high = values.astype(jnp.bfloat16)
    rest = values - high.astype(jnp.float32)
    mid = rest.astype(jnp.bfloat16)
    low = (rest - mid.astype(jnp.float32)).astype(jnp.bfloat16)
    return high, mid, low


def dot_t(a, b):
    return lax.dot_general(a, b, (((1,), (1,)), ((), ())), preferred_element_type=jnp.float32)


def up_y(v):
    return pltpu.roll(v, v.shape[0] - 1, 0)


def down_y(v):
    return pltpu.roll(v, 1, 0)


def up_z(v):
    return pltpu.roll(v, v.shape[1] - 1, 1)


def down_z(v):
    return pltpu.roll(v, 1, 1)


def source_slices(dx, dy, lx, ly):
    width = RIM if dy == 0 else 1
    if dx == 0:
        xs, xd = (0, lx), RIM
    elif dx > 0:
        xs, xd = (lx - width, width), RIM - width
    else:
        xs, xd = (0, width), lx + RIM
    if dy == 0:
        ys, yd = (0, ly), PAD
    elif dy > 0:
        ys, yd = (ly - PAD, PAD), 0
    else:
        ys, yd = (0, PAD), ly + PAD
    return xs, ys, xd, yd


def kernel(
    nx,
    ny,
    lc_ref,
    c_ref,
    survey_ref,
    weight_ref,
    wcell_ref,
    wdata_ref,
    wweight_ref,
    scell_ref,
    srate_ref,
    step_ref,
    grad_ref,
    adj_ref,
    conc_ref,
    misfit_ref,
    h,
    c0,
    c1,
    a2,
    a1,
    fu,
    fl,
    ky,
    kz,
    q,
    ww,
    wd,
    sv,
    sw,
    red_y,
    red_x,
    local_sem,
    send1,
    recv1,
    send2,
    recv2,
    send_y,
    recv_y,
    send_x,
    recv_x,
):
    f32 = jnp.float32
    lx, ly, nz = c_ref.shape
    rows = ly + 2 * PAD
    i = lax.axis_index("gx")
    j = lax.axis_index("gy")
    body = (slice(None), pl.ds(PAD, ly), slice(None))

    loads = [
        pltpu.make_async_copy(lc_ref, h.at[pl.ds(RIM, lx), pl.ds(PAD, ly)], local_sem.at[0]),
        pltpu.make_async_copy(c_ref, c0.at[pl.ds(RIM, lx), pl.ds(PAD, ly)], local_sem.at[1]),
        pltpu.make_async_copy(survey_ref, sv, local_sem.at[2]),
        pltpu.make_async_copy(weight_ref, sw, local_sem.at[3]),
    ]

    def inside(a, b):
        return (a >= 0) & (a < nx) & (b >= 0) & (b < ny)

    barrier = pltpu.get_barrier_semaphore()

    def greet(di, dj):
        pl.semaphore_signal(barrier, inc=1, device_id={"gx": di, "gy": dj}, device_id_type=MESH)

    for dx, dy in DIRS[4:]:

        @pl.when(inside(i + dx, j + dy))
        def _():
            greet(i + dx, j + dy)

    @pl.loop(1, nx)
    def _(o):
        greet(lax.rem(i + o, nx), j)

    @pl.loop(1, ny)
    def _(o):
        greet(i, lax.rem(j + o, ny))

    for load in loads:
        load.start()

    def one(flag):
        return jnp.where(flag, 1, 0)

    sides = (one(i > 0) + one(i < nx - 1)) * (one(j > 0) + one(j < ny - 1))
    pl.semaphore_wait(barrier, nx - 1 + ny - 1 + sides)

    def remote(d, src, dst, off_x, off_y, send, recv):
        dx, dy = DIRS[d]
        xs, ys, xd, yd = source_slices(dx, dy, lx, ly)
        return pltpu.make_async_remote_copy(
            src_ref=src.at[pl.ds(xs[0] + off_x, xs[1]), pl.ds(ys[0] + off_y, ys[1])],
            dst_ref=dst.at[pl.ds(xd, xs[1]), pl.ds(yd, ys[1])],
            send_sem=send,
            recv_sem=recv,
            device_id={"gx": i + dx, "gy": j + dy},
            device_id_type=MESH,
        )

    first = [
        [
            remote(d, c_ref, c0, 0, 0, send1.at[2 * d], recv1.at[2 * d]),
            remote(d, lc_ref, h, 0, 0, send1.at[2 * d + 1], recv1.at[2 * d + 1]),
        ]
        for d in range(8)
    ]
    second = [[remote(d, a2, a2, RIM, PAD, send2.at[d], recv2.at[d])] for d in range(8)]

    def start(copies, d):
        dx, dy = DIRS[d]

        @pl.when(inside(i + dx, j + dy))
        def _():
            for copy in copies[d]:
                copy.start()

    def arrive(copies, d):
        dx, dy = DIRS[d]

        @pl.when(inside(i - dx, j - dy))
        def _():
            for copy in copies[d]:
                copy.wait_recv()

    def sent(copies, d):
        dx, dy = DIRS[d]

        @pl.when(inside(i + dx, j + dy))
        def _():
            for copy in copies[d]:
                copy.wait_send()

    for d in (2, 3, 4, 5, 6, 7, 0, 1):
        start(first, d)

    def fill(d, refs):
        dx, dy = DIRS[d]
        xs, ys, xd, yd = source_slices(dx, dy, lx, ly)

        @pl.when(jnp.logical_not(inside(i - dx, j - dy)))
        def _():
            for ref in refs:
                ref[pl.ds(xd, xs[1]), pl.ds(yd, ys[1])] = jnp.zeros((xs[1], ys[1], nz), f32)

    for d in range(8):
        fill(d, (c0, h, a2))
    for ref in (c0, h, a2):
        for x in (0, lx + 2 * RIM - 1):
            for y in (0, ly + PAD):
                ref[x, pl.ds(y, PAD)] = jnp.zeros((PAD, nz), f32)

    grid_y = ly * ny
    wcell = wcell_ref[...].reshape(1, -1)
    scell = scell_ref[...].reshape(1, -1)
    wweight = wweight_ref[...].reshape(1, -1)
    wdata = wdata_ref[...].reshape(1, -1)
    srate = srate_ref[...].reshape(1, -1)
    nobs, nsrc = wcell.shape[1], scell.shape[1]
    zi = lax.broadcasted_iota(jnp.int32, (nz, nobs), 0)
    at_z = zi == lax.rem(wcell, nz)
    well_parts = []
    for part_w, part_d in zip(split3(wweight), split3(wweight * wdata)):
        both = [jnp.where(at_z, p.astype(f32), 0.0).astype(jnp.bfloat16) for p in (part_w, part_d)]
        well_parts.append(jnp.concatenate(both, axis=0))
    src_z = lax.broadcasted_iota(jnp.int32, (nz, nsrc), 0) == lax.rem(scell, nz)
    src_parts = [jnp.where(src_z, p.astype(f32), 0.0).astype(jnp.bfloat16) for p in split3(srate)]
    src_parts = jnp.concatenate(src_parts, axis=0)
    well_row = lax.div(wcell, nz) - (i * lx * grid_y + j * ly)
    src_row = lax.div(scell, nz) - (i * lx * grid_y + j * ly)
    well_iota = lax.broadcasted_iota(jnp.int32, (ly, nobs), 0)
    src_iota = lax.broadcasted_iota(jnp.int32, (rows, nsrc), 0) - PAD

    @pl.loop(0, lx)
    def _(x):
        hot = jnp.where(well_iota == well_row - x * grid_y, 1.0, 0.0).astype(jnp.bfloat16)
        both = dot_t(hot, well_parts[0]) + dot_t(hot, well_parts[1]) + dot_t(hot, well_parts[2])
        ww[x] = both[:, :nz]
        wd[x] = both[:, nz:]

    @pl.loop(0, lx + 2)
    def _(x):
        hot = jnp.where(src_iota == src_row - (x - 1) * grid_y, 1.0, 0.0).astype(jnp.bfloat16)
        parts = dot_t(hot, src_parts)
        q[x] = parts[:, :nz] + parts[:, nz : 2 * nz] + parts[:, 2 * nz :]

    clock = jnp.full((1, nz), step_ref[0], jnp.int32).astype(f32)
    gain_first = time_step * (1.0 + 0.5 * jnp.sin(0.05 * clock))
    gain_second = time_step * (1.0 + 0.5 * jnp.sin(0.05 * (clock + 1.0)))

    lane = lax.broadcasted_iota(jnp.int32, (rows, nz), 1)
    row = lax.broadcasted_iota(jnp.int32, (rows, nz), 0)
    low_face = jnp.where(j == 0, PAD - 1, -1)
    high_face = jnp.where(j == ny - 1, PAD + ly - 1, -1)

    def faces_in(x):
        open_z = lane < nz - 1
        open_y = (row != low_face) & (row != high_face)
        half = h[x]
        ky[x] = jnp.where(
            open_y, time_step * molecular + time_step * dispersivity * (half * up_y(half)), 0.0
        )
        kz[x] = jnp.where(
            open_z, time_step * molecular + time_step * dispersivity * (half * up_z(half)), 0.0
        )

    def root(x):
        h[x] = jnp.exp(0.5 * h[x])

    def faces_x(x):
        cond = time_step * (h[x] * h[x + 1])
        closed = ((i == 0) & (x == RIM - 1)) | ((i == nx - 1) & (x == RIM + lx - 1))
        keep = jnp.where(closed, 0.0, 1.0)
        fu[x] = keep * (time_step * molecular + (head_slope + dispersivity) * cond)
        fl[x] = keep * (time_step * molecular + dispersivity * cond)

    def spread_yz(v, x):
        gy = ky[x] * (up_y(v) - v)
        gz = kz[x] * (up_z(v) - v)
        return (gy - down_y(gy)) + (gz - down_z(gz))

    def forward(src, x):
        v = src[x]
        out = fu[x] * v - fl[x] * src[x + 1]
        into = fu[x - 1] * src[x - 1] - fl[x - 1] * v
        return v + ((into - out) + spread_yz(v, x))

    def backward(src, x):
        v = src[x]
        above = src[x + 1] - v
        below = v - src[x - 1]
        return v + ((above * fu[x] - below * fl[x - 1]) + spread_yz(v, x))

    def do_c1(x):
        c1[x] = forward(c0, x) + gain_first * q[x - 1]

    def do_c2(x, total):
        final = (forward(c1, x) + gain_second * q[x - 1])[PAD : PAD + ly]
        b = x - RIM
        conc_ref[b] = final
        missed = final - sv[b]
        seed = sw[b] * missed
        heavy = ww[b] * final
        pulled = wd[b]
        a2[x, pl.ds(PAD, ly)] = seed + (heavy - pulled)
        term = seed * missed + final * (heavy - 2.0 * pulled)
        return total + jnp.sum(term.reshape(ly // 8, 8, nz), axis=0)

    def do_a1(x):
        a1[x] = backward(a2, x)

    def do_out(x):
        b = x - RIM
        v1, v2 = a1[x], a2[x]
        t0, t1 = c0[x], c1[x]
        lean = (head_slope + dispersivity)

        def face_x(p):
            low1 = lean * c1[p] - dispersivity * c1[p + 1]
            low0 = lean * c0[p] - dispersivity * c0[p + 1]
            d1 = a1[p + 1] - a1[p]
            d2 = a2[p + 1] - a2[p]
            return (fu[p] - fl[p]) * (d2 * low1 + d1 * low0), d1

        gx_up, above = face_x(x)
        gx_low, below = face_x(x - 1)
        grad = gx_up + gx_low
        new = v1 + (above * fu[x] - below * fl[x - 1])
        for k, up, down in ((ky[x], up_y, down_y), (kz[x], up_z, down_z)):
            d1 = up(v1) - v1
            flow = k * d1
            new = new + (flow - down(flow))
            sens = (d1 * (up(t0) - t0) + (up(v2) - v2) * (up(t1) - t1)) * (
                -0.5 * jnp.maximum(k - time_step * molecular, 0.0)
            )
            grad = grad + (sens + down(sens))
        grad_ref[b] = grad[PAD : PAD + ly]
        adj_ref[b] = new[PAD : PAD + ly]

    def loop(low, high, f):
        @pl.loop(low, high)
        def _(x):
            f(x)

    lo, hi = RIM, RIM + lx
    for load in loads:
        load.wait()
    arrive(first, 2)
    arrive(first, 3)
    loop(lo, hi, root)
    loop(lo, hi, faces_in)
    loop(lo, hi - 1, faces_x)
    loop(lo + 1, hi - 1, do_c1)
    total = lax.fori_loop(lo + 2, hi - 2, do_c2, jnp.zeros((8, nz), f32))

    for d in (0, 1, 4, 5, 6, 7):
        arrive(first, d)
    for x in (lo - 2, lo - 1, hi, hi + 1):
        root(x)
    for x in (lo - 1, hi):
        faces_in(x)
    for x in (lo - 2, lo - 1, hi - 1, hi):
        faces_x(x)
    for x in (lo - 1, lo, hi - 1, hi):
        do_c1(x)
    for x in (lo, hi - 1, lo + 1, hi - 2):
        total = do_c2(x, total)

    for d in (0, 1, 2, 3, 4, 5, 6, 7):
        start(second, d)

    def reduce_start(ref, axis, me, count, send, recv):
        @pl.loop(1, count)
        def _(o):
            pltpu.make_async_remote_copy(
                src_ref=ref.at[me],
                dst_ref=ref.at[me],
                send_sem=send.at[o],
                recv_sem=recv.at[me],
                device_id={axis: lax.rem(me + o, count)},
                device_id_type=MESH,
            ).start()

    def reduce_wait(ref, axis, me, count, send, recv):
        @pl.loop(1, count)
        def _(o):
            other = lax.rem(me + o, count)
            copy = pltpu.make_async_remote_copy(
                src_ref=ref.at[me],
                dst_ref=ref.at[other],
                send_sem=send.at[o],
                recv_sem=recv.at[other],
                device_id={axis: other},
                device_id_type=MESH,
            )
            copy.wait_send()
            copy.wait_recv()

    red_y[j] = total
    reduce_start(red_y, "gy", j, ny, send_y, recv_y)

    for d in (2, 3):
        arrive(second, d)
    loop(lo + 2, hi - 2, do_a1)

    reduce_wait(red_y, "gy", j, ny, send_y, recv_y)
    red_x[i] = jnp.sum(red_y[...], axis=0)
    reduce_start(red_x, "gx", i, nx, send_x, recv_x)

    do_a1(lo + 1)
    do_a1(hi - 2)
    loop(lo + 2, hi - 2, do_out)

    for d in (0, 1, 4, 5, 6, 7):
        arrive(second, d)
    for x in (lo - 1, lo, hi - 1, hi):
        do_a1(x)
    for x in (lo, lo + 1, hi - 2, hi - 1):
        do_out(x)

    reduce_wait(red_x, "gx", i, nx, send_x, recv_x)
    wells = jnp.sum(wweight * wdata * wdata)
    whole = jnp.sum(jnp.sum(red_x[...], axis=0)) + wells
    misfit_ref[0] = whole * (0.5 / (nx * lx * grid_y * nz))
    for d in range(8):
        sent(first, d)
        sent(second, d)


def on_device(*args):
    lx, ly, nz = args[1].shape
    nx = lax.axis_size("gx")
    ny = lax.axis_size("gy")
    rows = ly + 2 * PAD
    wide = pltpu.VMEM((lx + 2 * RIM, rows, nz), jnp.float32)
    block = pltpu.VMEM((lx, ly, nz), jnp.float32)
    field = jax.ShapeDtypeStruct((lx, ly, nz), jnp.float32)
    anywhere = pl.BlockSpec(memory_space=pl.ANY)
    vmem = pl.BlockSpec(memory_space=pltpu.VMEM)
    smem = pl.BlockSpec(memory_space=pltpu.SMEM)
    dma = pltpu.SemaphoreType.DMA
    return pl.pallas_call(
        functools.partial(kernel, nx, ny),
        out_shape=(field, field, field, jax.ShapeDtypeStruct((1,), jnp.float32)),
        in_specs=[anywhere] * 4 + [vmem] * 5 + [smem],
        out_specs=(vmem, vmem, vmem, smem),
        scratch_shapes=[wide] * 9
        + [pltpu.VMEM((lx + 2, rows, nz), jnp.float32)]
        + [block] * 4
        + [pltpu.VMEM((ny, 8, nz), jnp.float32), pltpu.VMEM((nx, 8, nz), jnp.float32)]
        + [dma((4,)), dma((16,)), dma((16,)), dma((8,)), dma((8,))]
        + [dma((ny,)), dma((ny,)), dma((nx,)), dma((nx,))],
        compiler_params=pltpu.CompilerParams(
            collective_id=0, has_side_effects=True, vmem_limit_bytes=40 * 1024 * 1024
        ),
    )(*args)


def solution(mesh):
    return jax.shard_map(
        on_device,
        mesh=mesh,
        in_specs=(P(("ens", "gx"), "gy", None),) * 4 + (P("ens"),) * 6,
        out_specs=(P(("ens", "gx"), "gy", None),) * 3 + (P("ens"),),
        check_vma=False,
    )
```

```python
import functools

import jax
import jax.numpy as jnp
from jax import lax
from jax.experimental import pallas as pl
from jax.experimental.pallas import tpu as pltpu
from jax.sharding import PartitionSpec as P

time_step = 0.2
head_slope = 0.5
molecular = 0.05
dispersivity = 0.1

RIM = 2
PAD = 8
DIRS = ((1, 0), (-1, 0), (0, 1), (0, -1), (1, 1), (1, -1), (-1, 1), (-1, -1))
MESH = pl.DeviceIdType.MESH


def split3(values):
    high = values.astype(jnp.bfloat16)
    rest = values - high.astype(jnp.float32)
    mid = rest.astype(jnp.bfloat16)
    low = (rest - mid.astype(jnp.float32)).astype(jnp.bfloat16)
    return high, mid, low


def dot_t(a, b):
    return lax.dot_general(a, b, (((1,), (1,)), ((), ())), preferred_element_type=jnp.float32)


def up_y(v):
    return pltpu.roll(v, v.shape[0] - 1, 0)


def down_y(v):
    return pltpu.roll(v, 1, 0)


def up_z(v):
    return pltpu.roll(v, v.shape[1] - 1, 1)


def down_z(v):
    return pltpu.roll(v, 1, 1)


def source_slices(dx, dy, lx, ly):
    width = RIM if dy == 0 else 1
    if dx == 0:
        xs, xd = (0, lx), RIM
    elif dx > 0:
        xs, xd = (lx - width, width), RIM - width
    else:
        xs, xd = (0, width), lx + RIM
    if dy == 0:
        ys, yd = (0, ly), PAD
    elif dy > 0:
        ys, yd = (ly - PAD, PAD), 0
    else:
        ys, yd = (0, PAD), ly + PAD
    return xs, ys, xd, yd


def kernel(
    nx,
    ny,
    lc_ref,
    c_ref,
    survey_ref,
    weight_ref,
    wcell_hbm,
    wdata_hbm,
    wweight_hbm,
    scell_hbm,
    srate_hbm,
    step_ref,
    grad_ref,
    adj_ref,
    conc_ref,
    misfit_ref,
    h,
    c0,
    c1,
    a2,
    a1,
    fu,
    fl,
    ky,
    kz,
    q,
    ww,
    wd,
    sv,
    sw,
    wcell_ref,
    wdata_ref,
    wweight_ref,
    scell_ref,
    srate_ref,
    red_y,
    red_x,
    local_sem,
    send1,
    recv1,
    send2,
    recv2,
    send_y,
    recv_y,
    send_x,
    recv_x,
):
    f32 = jnp.float32
    lx, ly, nz = c_ref.shape
    rows = ly + 2 * PAD
    i = lax.axis_index("gx")
    j = lax.axis_index("gy")
    body = (slice(None), pl.ds(PAD, ly), slice(None))

    loads = [
        pltpu.make_async_copy(lc_ref, h.at[pl.ds(RIM, lx), pl.ds(PAD, ly)], local_sem.at[0]),
        pltpu.make_async_copy(c_ref, c0.at[pl.ds(RIM, lx), pl.ds(PAD, ly)], local_sem.at[1]),
        pltpu.make_async_copy(survey_ref, sv, local_sem.at[2]),
        pltpu.make_async_copy(weight_ref, sw, local_sem.at[3]),
    ]

    small = [
        pltpu.make_async_copy(src, dst, local_sem.at[4 + k])
        for k, (src, dst) in enumerate(
            (
                (wcell_hbm, wcell_ref),
                (wdata_hbm, wdata_ref),
                (wweight_hbm, wweight_ref),
                (scell_hbm, scell_ref),
                (srate_hbm, srate_ref),
            )
        )
    ]

    def inside(a, b):
        return (a >= 0) & (a < nx) & (b >= 0) & (b < ny)

    barrier = pltpu.get_barrier_semaphore()

    def greet(di, dj):
        pl.semaphore_signal(barrier, inc=1, device_id={"gx": di, "gy": dj}, device_id_type=MESH)

    for dx, dy in DIRS[4:]:

        @pl.when(inside(i + dx, j + dy))
        def _():
            greet(i + dx, j + dy)

    @pl.loop(1, nx)
    def _(o):
        greet(lax.rem(i + o, nx), j)

    @pl.loop(1, ny)
    def _(o):
        greet(i, lax.rem(j + o, ny))

    for load in small + loads:
        load.start()

    def one(flag):
        return jnp.where(flag, 1, 0)

    sides = (one(i > 0) + one(i < nx - 1)) * (one(j > 0) + one(j < ny - 1))
    pl.semaphore_wait(barrier, nx - 1 + ny - 1 + sides)

    def remote(d, src, dst, off_x, off_y, send, recv):
        dx, dy = DIRS[d]
        xs, ys, xd, yd = source_slices(dx, dy, lx, ly)
        return pltpu.make_async_remote_copy(
            src_ref=src.at[pl.ds(xs[0] + off_x, xs[1]), pl.ds(ys[0] + off_y, ys[1])],
            dst_ref=dst.at[pl.ds(xd, xs[1]), pl.ds(yd, ys[1])],
            send_sem=send,
            recv_sem=recv,
            device_id={"gx": i + dx, "gy": j + dy},
            device_id_type=MESH,
        )

    first = [
        [
            remote(d, c_ref, c0, 0, 0, send1.at[2 * d], recv1.at[2 * d]),
            remote(d, lc_ref, h, 0, 0, send1.at[2 * d + 1], recv1.at[2 * d + 1]),
        ]
        for d in range(8)
    ]
    second = [[remote(d, a2, a2, RIM, PAD, send2.at[d], recv2.at[d])] for d in range(8)]

    def start(copies, d):
        dx, dy = DIRS[d]

        @pl.when(inside(i + dx, j + dy))
        def _():
            for copy in copies[d]:
                copy.start()

    def arrive(copies, d):
        dx, dy = DIRS[d]

        @pl.when(inside(i - dx, j - dy))
        def _():
            for copy in copies[d]:
                copy.wait_recv()

    def sent(copies, d):
        dx, dy = DIRS[d]

        @pl.when(inside(i + dx, j + dy))
        def _():
            for copy in copies[d]:
                copy.wait_send()

    for d in (2, 3, 4, 5, 6, 7, 0, 1):
        start(first, d)

    def fill(d, refs):
        dx, dy = DIRS[d]
        xs, ys, xd, yd = source_slices(dx, dy, lx, ly)

        @pl.when(jnp.logical_not(inside(i - dx, j - dy)))
        def _():
            for ref in refs:
                ref[pl.ds(xd, xs[1]), pl.ds(yd, ys[1])] = jnp.zeros((xs[1], ys[1], nz), f32)

    for d in range(8):
        fill(d, (c0, h, a2))
    for ref in (c0, h, a2):
        for x in (0, lx + 2 * RIM - 1):
            for y in (0, ly + PAD):
                ref[x, pl.ds(y, PAD)] = jnp.zeros((PAD, nz), f32)

    for load in small:
        load.wait()
    grid_y = ly * ny
    wcell = wcell_ref[...].reshape(1, -1)
    scell = scell_ref[...].reshape(1, -1)
    wweight = wweight_ref[...].reshape(1, -1)
    wdata = wdata_ref[...].reshape(1, -1)
    srate = srate_ref[...].reshape(1, -1)
    nobs, nsrc = wcell.shape[1], scell.shape[1]
    zi = lax.broadcasted_iota(jnp.int32, (nz, nobs), 0)
    at_z = zi == lax.rem(wcell, nz)
    well_parts = []
    for part_w, part_d in zip(split3(wweight), split3(wweight * wdata)):
        both = [jnp.where(at_z, p.astype(f32), 0.0).astype(jnp.bfloat16) for p in (part_w, part_d)]
        well_parts.append(jnp.concatenate(both, axis=0))
    src_z = lax.broadcasted_iota(jnp.int32, (nz, nsrc), 0) == lax.rem(scell, nz)
    src_parts = [jnp.where(src_z, p.astype(f32), 0.0).astype(jnp.bfloat16) for p in split3(srate)]
    src_parts = jnp.concatenate(src_parts, axis=0)
    well_row = lax.div(wcell, nz) - (i * lx * grid_y + j * ly)
    src_row = lax.div(scell, nz) - (i * lx * grid_y + j * ly)
    well_iota = lax.broadcasted_iota(jnp.int32, (ly, nobs), 0)
    src_iota = lax.broadcasted_iota(jnp.int32, (rows, nsrc), 0) - PAD

    @pl.loop(0, lx)
    def _(x):
        hot = jnp.where(well_iota == well_row - x * grid_y, 1.0, 0.0).astype(jnp.bfloat16)
        both = dot_t(hot, well_parts[0]) + dot_t(hot, well_parts[1]) + dot_t(hot, well_parts[2])
        ww[x] = both[:, :nz]
        wd[x] = both[:, nz:]

    @pl.loop(0, lx + 2)
    def _(x):
        hot = jnp.where(src_iota == src_row - (x - 1) * grid_y, 1.0, 0.0).astype(jnp.bfloat16)
        parts = dot_t(hot, src_parts)
        q[x] = parts[:, :nz] + parts[:, nz : 2 * nz] + parts[:, 2 * nz :]

    clock = jnp.full((1, nz), step_ref[0], jnp.int32).astype(f32)
    gain_first = time_step * (1.0 + 0.5 * jnp.sin(0.05 * clock))
    gain_second = time_step * (1.0 + 0.5 * jnp.sin(0.05 * (clock + 1.0)))

    lane = lax.broadcasted_iota(jnp.int32, (rows, nz), 1)
    row = lax.broadcasted_iota(jnp.int32, (rows, nz), 0)
    low_face = jnp.where(j == 0, PAD - 1, -1)
    high_face = jnp.where(j == ny - 1, PAD + ly - 1, -1)

    def faces_in(x):
        open_z = lane < nz - 1
        open_y = (row != low_face) & (row != high_face)
        half = h[x]
        ky[x] = jnp.where(
            open_y, time_step * molecular + time_step * dispersivity * (half * up_y(half)), 0.0
        )
        kz[x] = jnp.where(
            open_z, time_step * molecular + time_step * dispersivity * (half * up_z(half)), 0.0
        )

    def root(x):
        h[x] = jnp.exp(0.5 * h[x])

    def faces_x(x):
        cond = time_step * (h[x] * h[x + 1])
        closed = ((i == 0) & (x == RIM - 1)) | ((i == nx - 1) & (x == RIM + lx - 1))
        keep = jnp.where(closed, 0.0, 1.0)
        fu[x] = keep * (time_step * molecular + (head_slope + dispersivity) * cond)
        fl[x] = keep * (time_step * molecular + dispersivity * cond)

    def spread_yz(v, x):
        gy = ky[x] * (up_y(v) - v)
        gz = kz[x] * (up_z(v) - v)
        return (gy - down_y(gy)) + (gz - down_z(gz))

    def forward(src, x):
        v = src[x]
        out = fu[x] * v - fl[x] * src[x + 1]
        into = fu[x - 1] * src[x - 1] - fl[x - 1] * v
        return v + ((into - out) + spread_yz(v, x))

    def backward(src, x):
        v = src[x]
        above = src[x + 1] - v
        below = v - src[x - 1]
        return v + ((above * fu[x] - below * fl[x - 1]) + spread_yz(v, x))

    def do_c1(x):
        c1[x] = forward(c0, x) + gain_first * q[x - 1]

    def do_c2(x, total):
        final = (forward(c1, x) + gain_second * q[x - 1])[PAD : PAD + ly]
        b = x - RIM
        conc_ref[b] = final
        missed = final - sv[b]
        seed = sw[b] * missed
        heavy = ww[b] * final
        pulled = wd[b]
        a2[x, pl.ds(PAD, ly)] = seed + (heavy - pulled)
        term = seed * missed + final * (heavy - 2.0 * pulled)
        return total + jnp.sum(term.reshape(ly // 8, 8, nz), axis=0)

    def do_a1(x):
        a1[x] = backward(a2, x)

    def do_out(x):
        b = x - RIM
        v1, v2 = a1[x], a2[x]
        t0, t1 = c0[x], c1[x]
        lean = (head_slope + dispersivity)

        def face_x(p):
            low1 = lean * c1[p] - dispersivity * c1[p + 1]
            low0 = lean * c0[p] - dispersivity * c0[p + 1]
            d1 = a1[p + 1] - a1[p]
            d2 = a2[p + 1] - a2[p]
            return (fu[p] - fl[p]) * (d2 * low1 + d1 * low0), d1

        gx_up, above = face_x(x)
        gx_low, below = face_x(x - 1)
        grad = gx_up + gx_low
        new = v1 + (above * fu[x] - below * fl[x - 1])
        for k, up, down in ((ky[x], up_y, down_y), (kz[x], up_z, down_z)):
            d1 = up(v1) - v1
            flow = k * d1
            new = new + (flow - down(flow))
            sens = (d1 * (up(t0) - t0) + (up(v2) - v2) * (up(t1) - t1)) * (
                -0.5 * jnp.maximum(k - time_step * molecular, 0.0)
            )
            grad = grad + (sens + down(sens))
        grad_ref[b] = grad[PAD : PAD + ly]
        adj_ref[b] = new[PAD : PAD + ly]

    def loop(low, high, f):
        @pl.loop(low, high)
        def _(x):
            f(x)

    lo, hi = RIM, RIM + lx
    for load in loads:
        load.wait()
    arrive(first, 2)
    arrive(first, 3)
    loop(lo, hi, root)
    loop(lo, hi, faces_in)
    loop(lo, hi - 1, faces_x)
    loop(lo + 1, hi - 1, do_c1)
    total = lax.fori_loop(lo + 2, hi - 2, do_c2, jnp.zeros((8, nz), f32))

    for d in (0, 1, 4, 5, 6, 7):
        arrive(first, d)
    for x in (lo - 2, lo - 1, hi, hi + 1):
        root(x)
    for x in (lo - 1, hi):
        faces_in(x)
    for x in (lo - 2, lo - 1, hi - 1, hi):
        faces_x(x)
    for x in (lo - 1, lo, hi - 1, hi):
        do_c1(x)
    for x in (lo, hi - 1, lo + 1, hi - 2):
        total = do_c2(x, total)

    for d in (0, 1, 2, 3, 4, 5, 6, 7):
        start(second, d)

    def reduce_start(ref, axis, me, count, send, recv):
        @pl.loop(1, count)
        def _(o):
            pltpu.make_async_remote_copy(
                src_ref=ref.at[me],
                dst_ref=ref.at[me],
                send_sem=send.at[o],
                recv_sem=recv.at[me],
                device_id={axis: lax.rem(me + o, count)},
                device_id_type=MESH,
            ).start()

    def reduce_wait(ref, axis, me, count, send, recv):
        @pl.loop(1, count)
        def _(o):
            other = lax.rem(me + o, count)
            copy = pltpu.make_async_remote_copy(
                src_ref=ref.at[me],
                dst_ref=ref.at[other],
                send_sem=send.at[o],
                recv_sem=recv.at[other],
                device_id={axis: other},
                device_id_type=MESH,
            )
            copy.wait_send()
            copy.wait_recv()

    red_y[j] = total
    reduce_start(red_y, "gy", j, ny, send_y, recv_y)

    for d in (2, 3):
        arrive(second, d)
    loop(lo + 2, hi - 2, do_a1)

    reduce_wait(red_y, "gy", j, ny, send_y, recv_y)
    red_x[i] = jnp.sum(red_y[...], axis=0)
    reduce_start(red_x, "gx", i, nx, send_x, recv_x)

    do_a1(lo + 1)
    do_a1(hi - 2)
    loop(lo + 2, hi - 2, do_out)

    for d in (0, 1, 4, 5, 6, 7):
        arrive(second, d)
    for x in (lo - 1, lo, hi - 1, hi):
        do_a1(x)
    for x in (lo, lo + 1, hi - 2, hi - 1):
        do_out(x)

    reduce_wait(red_x, "gx", i, nx, send_x, recv_x)
    wells = jnp.sum(wweight * wdata * wdata)
    whole = jnp.sum(jnp.sum(red_x[...], axis=0)) + wells
    misfit_ref[0] = whole * (0.5 / (nx * lx * grid_y * nz))
    for d in range(8):
        sent(first, d)
        sent(second, d)


def on_device(*args):
    lx, ly, nz = args[1].shape
    nx = lax.axis_size("gx")
    ny = lax.axis_size("gy")
    rows = ly + 2 * PAD
    wide = pltpu.VMEM((lx + 2 * RIM, rows, nz), jnp.float32)
    block = pltpu.VMEM((lx, ly, nz), jnp.float32)
    field = jax.ShapeDtypeStruct((lx, ly, nz), jnp.float32)
    hbm = pl.BlockSpec(memory_space=pltpu.HBM)
    vmem = pl.BlockSpec(memory_space=pltpu.VMEM)
    smem = pl.BlockSpec(memory_space=pltpu.SMEM)
    dma = pltpu.SemaphoreType.DMA
    return pl.pallas_call(
        functools.partial(kernel, nx, ny),
        out_shape=(field, field, field, jax.ShapeDtypeStruct((1,), jnp.float32)),
        in_specs=[hbm] * 9 + [smem],
        out_specs=(vmem, vmem, vmem, smem),
        scratch_shapes=[wide] * 9
        + [pltpu.VMEM((lx + 2, rows, nz), jnp.float32)]
        + [block] * 4
        + [pltpu.VMEM(a.shape, a.dtype) for a in args[4:9]]
        + [pltpu.VMEM((ny, 8, nz), jnp.float32), pltpu.VMEM((nx, 8, nz), jnp.float32)]
        + [dma((9,)), dma((16,)), dma((16,)), dma((8,)), dma((8,))]
        + [dma((ny,)), dma((ny,)), dma((nx,)), dma((nx,))],
        compiler_params=pltpu.CompilerParams(
            collective_id=0, has_side_effects=True, vmem_limit_bytes=40 * 1024 * 1024
        ),
    )(*args)


def solution(mesh):
    return jax.shard_map(
        on_device,
        mesh=mesh,
        in_specs=(P(("ens", "gx"), "gy", None),) * 4 + (P("ens"),) * 6,
        out_specs=(P(("ens", "gx"), "gy", None),) * 3 + (P("ens"),),
        check_vma=False,
    )
```

```python
import functools

import jax
import jax.numpy as jnp
from jax import lax
from jax.experimental import pallas as pl
from jax.experimental.pallas import tpu as pltpu
from jax.sharding import PartitionSpec as P

time_step = 0.2
head_slope = 0.5
molecular = 0.05
dispersivity = 0.1

RIM = 2
PAD = 8
DIRS = ((1, 0), (-1, 0), (0, 1), (0, -1), (1, 1), (1, -1), (-1, 1), (-1, -1))
MESH = pl.DeviceIdType.MESH


def split3(values):
    high = values.astype(jnp.bfloat16)
    rest = values - high.astype(jnp.float32)
    mid = rest.astype(jnp.bfloat16)
    low = (rest - mid.astype(jnp.float32)).astype(jnp.bfloat16)
    return high, mid, low


def dot_t(a, b):
    return lax.dot_general(a, b, (((1,), (1,)), ((), ())), preferred_element_type=jnp.float32)


def up_y(v):
    return pltpu.roll(v, v.shape[0] - 1, 0)


def down_y(v):
    return pltpu.roll(v, 1, 0)


def up_z(v):
    return pltpu.roll(v, v.shape[1] - 1, 1)


def down_z(v):
    return pltpu.roll(v, 1, 1)


def source_slices(dx, dy, lx, ly):
    width = RIM if dy == 0 else 1
    if dx == 0:
        xs, xd = (0, lx), RIM
    elif dx > 0:
        xs, xd = (lx - width, width), RIM - width
    else:
        xs, xd = (0, width), lx + RIM
    if dy == 0:
        ys, yd = (0, ly), PAD
    elif dy > 0:
        ys, yd = (ly - PAD, PAD), 0
    else:
        ys, yd = (0, PAD), ly + PAD
    return xs, ys, xd, yd


def out_plane(x, c0, c1, a1, a2, fu, fl, ky, kz, ly):
    v1, v2 = a1[x], a2[x]
    t0, t1 = c0[x], c1[x]
    lean = head_slope + dispersivity

    def face_x(p):
        low1 = lean * c1[p] - dispersivity * c1[p + 1]
        low0 = lean * c0[p] - dispersivity * c0[p + 1]
        d1 = a1[p + 1] - a1[p]
        d2 = a2[p + 1] - a2[p]
        return (fu[p] - fl[p]) * (d2 * low1 + d1 * low0), d1

    gx_up, above = face_x(x)
    gx_low, below = face_x(x - 1)
    grad = gx_up + gx_low
    new = v1 + (above * fu[x] - below * fl[x - 1])
    for k, up, down in ((ky[x], up_y, down_y), (kz[x], up_z, down_z)):
        d1 = up(v1) - v1
        flow = k * d1
        new = new + (flow - down(flow))
        sens = (d1 * (up(t0) - t0) + (up(v2) - v2) * (up(t1) - t1)) * (
            -0.5 * jnp.maximum(k - time_step * molecular, 0.0)
        )
        grad = grad + (sens + down(sens))
    return grad[PAD : PAD + ly], new[PAD : PAD + ly]


def finish(c0, c1, a1, a2, fu, fl, ky, kz, grad_in, adj_in, conc_in, grad, adj, conc, edge, sems):
    lx, ly, nz = conc.shape
    mid = pl.ds(2, lx - 4)
    copies = [
        pltpu.make_async_copy(conc_in, conc, sems.at[0]),
        pltpu.make_async_copy(grad_in.at[mid], grad.at[mid], sems.at[1]),
        pltpu.make_async_copy(adj_in.at[mid], adj.at[mid], sems.at[2]),
    ]
    for copy in copies:
        copy.start()
    for k, b in enumerate((0, 1, lx - 2, lx - 1)):
        g, a = out_plane(b + RIM, c0, c1, a1, a2, fu, fl, ky, kz, ly)
        for slot, value, target in ((2 * k, g, grad), (2 * k + 1, a, adj)):
            edge[slot] = value
            copy = pltpu.make_async_copy(edge.at[slot], target.at[b], sems.at[3 + slot])
            copy.start()
            copies.append(copy)
    for copy in copies:
        copy.wait()


def kernel(
    nx,
    ny,
    lc_ref,
    c_ref,
    survey_ref,
    weight_ref,
    wcell_hbm,
    wdata_hbm,
    wweight_hbm,
    scell_hbm,
    srate_hbm,
    step_ref,
    c0,
    c1,
    a1,
    a2,
    fu,
    fl,
    ky,
    kz,
    grad_ref,
    adj_ref,
    conc_ref,
    misfit_ref,
    h,
    q,
    ww,
    wd,
    sv,
    sw,
    wcell_ref,
    wdata_ref,
    wweight_ref,
    scell_ref,
    srate_ref,
    red_y,
    red_x,
    local_sem,
    send1,
    recv1,
    send2,
    recv2,
    send_y,
    recv_y,
    send_x,
    recv_x,
):
    f32 = jnp.float32
    lx, ly, nz = c_ref.shape
    rows = ly + 2 * PAD
    i = lax.axis_index("gx")
    j = lax.axis_index("gy")
    body = (slice(None), pl.ds(PAD, ly), slice(None))

    loads = [
        pltpu.make_async_copy(lc_ref, h.at[pl.ds(RIM, lx), pl.ds(PAD, ly)], local_sem.at[0]),
        pltpu.make_async_copy(c_ref, c0.at[pl.ds(RIM, lx), pl.ds(PAD, ly)], local_sem.at[1]),
        pltpu.make_async_copy(survey_ref, sv, local_sem.at[2]),
        pltpu.make_async_copy(weight_ref, sw, local_sem.at[3]),
    ]

    small = [
        pltpu.make_async_copy(src, dst, local_sem.at[4 + k])
        for k, (src, dst) in enumerate(
            (
                (wcell_hbm, wcell_ref),
                (wdata_hbm, wdata_ref),
                (wweight_hbm, wweight_ref),
                (scell_hbm, scell_ref),
                (srate_hbm, srate_ref),
            )
        )
    ]

    def inside(a, b):
        return (a >= 0) & (a < nx) & (b >= 0) & (b < ny)

    barrier = pltpu.get_barrier_semaphore()

    def greet(di, dj):
        pl.semaphore_signal(barrier, inc=1, device_id={"gx": di, "gy": dj}, device_id_type=MESH)

    for dx, dy in DIRS[4:]:

        @pl.when(inside(i + dx, j + dy))
        def _():
            greet(i + dx, j + dy)

    @pl.loop(1, nx)
    def _(o):
        greet(lax.rem(i + o, nx), j)

    @pl.loop(1, ny)
    def _(o):
        greet(i, lax.rem(j + o, ny))

    for load in small + loads:
        load.start()

    def one(flag):
        return jnp.where(flag, 1, 0)

    sides = (one(i > 0) + one(i < nx - 1)) * (one(j > 0) + one(j < ny - 1))
    pl.semaphore_wait(barrier, nx - 1 + ny - 1 + sides)

    def remote(d, src, dst, off_x, off_y, send, recv):
        dx, dy = DIRS[d]
        xs, ys, xd, yd = source_slices(dx, dy, lx, ly)
        return pltpu.make_async_remote_copy(
            src_ref=src.at[pl.ds(xs[0] + off_x, xs[1]), pl.ds(ys[0] + off_y, ys[1])],
            dst_ref=dst.at[pl.ds(xd, xs[1]), pl.ds(yd, ys[1])],
            send_sem=send,
            recv_sem=recv,
            device_id={"gx": i + dx, "gy": j + dy},
            device_id_type=MESH,
        )

    first = [
        [
            remote(d, c_ref, c0, 0, 0, send1.at[2 * d], recv1.at[2 * d]),
            remote(d, lc_ref, h, 0, 0, send1.at[2 * d + 1], recv1.at[2 * d + 1]),
        ]
        for d in range(8)
    ]
    second = [[remote(d, a2, a2, RIM, PAD, send2.at[d], recv2.at[d])] for d in range(8)]

    def start(copies, d):
        dx, dy = DIRS[d]

        @pl.when(inside(i + dx, j + dy))
        def _():
            for copy in copies[d]:
                copy.start()

    def arrive(copies, d):
        dx, dy = DIRS[d]

        @pl.when(inside(i - dx, j - dy))
        def _():
            for copy in copies[d]:
                copy.wait_recv()

    def sent(copies, d):
        dx, dy = DIRS[d]

        @pl.when(inside(i + dx, j + dy))
        def _():
            for copy in copies[d]:
                copy.wait_send()

    for d in (2, 3, 4, 5, 6, 7, 0, 1):
        start(first, d)

    def fill(d, refs):
        dx, dy = DIRS[d]
        xs, ys, xd, yd = source_slices(dx, dy, lx, ly)

        @pl.when(jnp.logical_not(inside(i - dx, j - dy)))
        def _():
            for ref in refs:
                ref[pl.ds(xd, xs[1]), pl.ds(yd, ys[1])] = jnp.zeros((xs[1], ys[1], nz), f32)

    for d in range(8):
        fill(d, (c0, h, a2))
    for ref in (c0, h, a2):
        for x in (0, lx + 2 * RIM - 1):
            for y in (0, ly + PAD):
                ref[x, pl.ds(y, PAD)] = jnp.zeros((PAD, nz), f32)

    for load in small:
        load.wait()
    grid_y = ly * ny
    wcell = wcell_ref[...].reshape(1, -1)
    scell = scell_ref[...].reshape(1, -1)
    wweight = wweight_ref[...].reshape(1, -1)
    wdata = wdata_ref[...].reshape(1, -1)
    srate = srate_ref[...].reshape(1, -1)
    nobs, nsrc = wcell.shape[1], scell.shape[1]
    zi = lax.broadcasted_iota(jnp.int32, (nz, nobs), 0)
    at_z = zi == lax.rem(wcell, nz)
    well_parts = []
    for part_w, part_d in zip(split3(wweight), split3(wweight * wdata)):
        both = [jnp.where(at_z, p.astype(f32), 0.0).astype(jnp.bfloat16) for p in (part_w, part_d)]
        well_parts.append(jnp.concatenate(both, axis=0))
    src_z = lax.broadcasted_iota(jnp.int32, (nz, nsrc), 0) == lax.rem(scell, nz)
    src_parts = [jnp.where(src_z, p.astype(f32), 0.0).astype(jnp.bfloat16) for p in split3(srate)]
    src_parts = jnp.concatenate(src_parts, axis=0)
    well_row = lax.div(wcell, nz) - (i * lx * grid_y + j * ly)
    src_row = lax.div(scell, nz) - (i * lx * grid_y + j * ly)
    well_iota = lax.broadcasted_iota(jnp.int32, (ly, nobs), 0)
    src_iota = lax.broadcasted_iota(jnp.int32, (rows, nsrc), 0) - PAD

    @pl.loop(0, lx)
    def _(x):
        hot = jnp.where(well_iota == well_row - x * grid_y, 1.0, 0.0).astype(jnp.bfloat16)
        both = dot_t(hot, well_parts[0]) + dot_t(hot, well_parts[1]) + dot_t(hot, well_parts[2])
        ww[x] = both[:, :nz]
        wd[x] = both[:, nz:]

    @pl.loop(0, lx + 2)
    def _(x):
        hot = jnp.where(src_iota == src_row - (x - 1) * grid_y, 1.0, 0.0).astype(jnp.bfloat16)
        parts = dot_t(hot, src_parts)
        q[x] = parts[:, :nz] + parts[:, nz : 2 * nz] + parts[:, 2 * nz :]

    clock = jnp.full((1, nz), step_ref[0], jnp.int32).astype(f32)
    gain_first = time_step * (1.0 + 0.5 * jnp.sin(0.05 * clock))
    gain_second = time_step * (1.0 + 0.5 * jnp.sin(0.05 * (clock + 1.0)))

    lane = lax.broadcasted_iota(jnp.int32, (rows, nz), 1)
    row = lax.broadcasted_iota(jnp.int32, (rows, nz), 0)
    low_face = jnp.where(j == 0, PAD - 1, -1)
    high_face = jnp.where(j == ny - 1, PAD + ly - 1, -1)

    def faces_in(x):
        open_z = lane < nz - 1
        open_y = (row != low_face) & (row != high_face)
        half = h[x]
        ky[x] = jnp.where(
            open_y, time_step * molecular + time_step * dispersivity * (half * up_y(half)), 0.0
        )
        kz[x] = jnp.where(
            open_z, time_step * molecular + time_step * dispersivity * (half * up_z(half)), 0.0
        )

    def root(x):
        h[x] = jnp.exp(0.5 * h[x])

    def faces_x(x):
        cond = time_step * (h[x] * h[x + 1])
        closed = ((i == 0) & (x == RIM - 1)) | ((i == nx - 1) & (x == RIM + lx - 1))
        keep = jnp.where(closed, 0.0, 1.0)
        fu[x] = keep * (time_step * molecular + (head_slope + dispersivity) * cond)
        fl[x] = keep * (time_step * molecular + dispersivity * cond)

    def spread_yz(v, x):
        gy = ky[x] * (up_y(v) - v)
        gz = kz[x] * (up_z(v) - v)
        return (gy - down_y(gy)) + (gz - down_z(gz))

    def forward(src, x):
        v = src[x]
        out = fu[x] * v - fl[x] * src[x + 1]
        into = fu[x - 1] * src[x - 1] - fl[x - 1] * v
        return v + ((into - out) + spread_yz(v, x))

    def backward(src, x):
        v = src[x]
        above = src[x + 1] - v
        below = v - src[x - 1]
        return v + ((above * fu[x] - below * fl[x - 1]) + spread_yz(v, x))

    def do_c1(x):
        c1[x] = forward(c0, x) + gain_first * q[x - 1]

    def do_c2(x, total):
        final = (forward(c1, x) + gain_second * q[x - 1])[PAD : PAD + ly]
        b = x - RIM
        conc_ref[b] = final
        missed = final - sv[b]
        seed = sw[b] * missed
        heavy = ww[b] * final
        pulled = wd[b]
        a2[x, pl.ds(PAD, ly)] = seed + (heavy - pulled)
        term = seed * missed + final * (heavy - 2.0 * pulled)
        return total + jnp.sum(term.reshape(ly // 8, 8, nz), axis=0)

    def do_a1(x):
        a1[x] = backward(a2, x)

    def do_out(x):
        g, a = out_plane(x, c0, c1, a1, a2, fu, fl, ky, kz, ly)
        grad_ref[x - RIM] = g
        adj_ref[x - RIM] = a

    def loop(low, high, f):
        @pl.loop(low, high)
        def _(x):
            f(x)

    lo, hi = RIM, RIM + lx
    for load in loads:
        load.wait()
    arrive(first, 2)
    arrive(first, 3)
    loop(lo, hi, root)
    loop(lo, hi, faces_in)
    loop(lo, hi - 1, faces_x)
    loop(lo + 1, hi - 1, do_c1)
    total = lax.fori_loop(lo + 2, hi - 2, do_c2, jnp.zeros((8, nz), f32))

    for d in (0, 1, 4, 5, 6, 7):
        arrive(first, d)
    for x in (lo - 2, lo - 1, hi, hi + 1):
        root(x)
    for x in (lo - 1, hi):
        faces_in(x)
    for x in (lo - 2, lo - 1, hi - 1, hi):
        faces_x(x)
    for x in (lo - 1, lo, hi - 1, hi):
        do_c1(x)
    for x in (lo, hi - 1, lo + 1, hi - 2):
        total = do_c2(x, total)

    for d in (0, 1, 2, 3, 4, 5, 6, 7):
        start(second, d)

    def reduce_start(ref, axis, me, count, send, recv):
        @pl.loop(1, count)
        def _(o):
            pltpu.make_async_remote_copy(
                src_ref=ref.at[me],
                dst_ref=ref.at[me],
                send_sem=send.at[o],
                recv_sem=recv.at[me],
                device_id={axis: lax.rem(me + o, count)},
                device_id_type=MESH,
            ).start()

    def reduce_wait(ref, axis, me, count, send, recv):
        @pl.loop(1, count)
        def _(o):
            other = lax.rem(me + o, count)
            copy = pltpu.make_async_remote_copy(
                src_ref=ref.at[me],
                dst_ref=ref.at[other],
                send_sem=send.at[o],
                recv_sem=recv.at[other],
                device_id={axis: other},
                device_id_type=MESH,
            )
            copy.wait_send()
            copy.wait_recv()

    red_y[j] = total
    reduce_start(red_y, "gy", j, ny, send_y, recv_y)

    for d in (2, 3):
        arrive(second, d)
    loop(lo + 2, hi - 2, do_a1)

    reduce_wait(red_y, "gy", j, ny, send_y, recv_y)
    red_x[i] = jnp.sum(red_y[...], axis=0)
    reduce_start(red_x, "gx", i, nx, send_x, recv_x)

    do_a1(lo + 1)
    do_a1(hi - 2)
    loop(lo + 2, hi - 2, do_out)

    for d in (0, 1, 4, 5, 6, 7):
        arrive(second, d)
    for x in (lo - 1, lo, hi - 1, hi):
        do_a1(x)

    reduce_wait(red_x, "gx", i, nx, send_x, recv_x)
    wells = jnp.sum(wweight * wdata * wdata)
    whole = jnp.sum(jnp.sum(red_x[...], axis=0)) + wells
    misfit_ref[0] = whole * (0.5 / (nx * lx * grid_y * nz))
    for d in range(8):
        sent(first, d)
        sent(second, d)


def on_device(*args):
    lx, ly, nz = args[1].shape
    nx = lax.axis_size("gx")
    ny = lax.axis_size("gy")
    rows = ly + 2 * PAD
    wide = (lx + 2 * RIM, rows, nz)
    block = (lx, ly, nz)
    hbm = pl.BlockSpec(memory_space=pltpu.HBM)
    vmem = pl.BlockSpec(memory_space=pltpu.VMEM)
    smem = pl.BlockSpec(memory_space=pltpu.SMEM)
    dma = pltpu.SemaphoreType.DMA
    f32 = jnp.float32
    pinned = [pltpu.with_memory_space_constraint(a, pltpu.HBM) for a in args[:9]]
    *fields, misfit = pl.pallas_call(
        functools.partial(kernel, nx, ny),
        out_shape=[pltpu.VMEM(wide, f32)] * 8
        + [pltpu.VMEM(block, f32)] * 3
        + [jax.ShapeDtypeStruct((1,), f32)],
        in_specs=[hbm] * 9 + [smem],
        out_specs=[vmem] * 11 + [smem],
        scratch_shapes=[pltpu.VMEM(wide, f32), pltpu.VMEM((lx + 2, rows, nz), f32)]
        + [pltpu.VMEM(block, f32)] * 4
        + [pltpu.VMEM(a.shape, a.dtype) for a in args[4:9]]
        + [pltpu.VMEM((ny, 8, nz), f32), pltpu.VMEM((nx, 8, nz), f32)]
        + [dma((9,)), dma((16,)), dma((16,)), dma((8,)), dma((8,))]
        + [dma((ny,)), dma((ny,)), dma((nx,)), dma((nx,))],
        compiler_params=pltpu.CompilerParams(
            collective_id=0, has_side_effects=True, vmem_limit_bytes=24 * 1024 * 1024
        ),
    )(*pinned, args[9])
    grad, adj, conc = pl.pallas_call(
        finish,
        out_shape=[pltpu.HBM(block, f32)] * 3,
        in_specs=[vmem] * 11,
        out_specs=[hbm] * 3,
        scratch_shapes=[pltpu.VMEM((8, ly, nz), f32), dma((11,))],
        compiler_params=pltpu.CompilerParams(vmem_limit_bytes=24 * 1024 * 1024),
    )(*fields)
    return grad, adj, conc, misfit


def solution(mesh):
    return jax.shard_map(
        on_device,
        mesh=mesh,
        in_specs=(P(("ens", "gx"), "gy", None),) * 4 + (P("ens"),) * 6,
        out_specs=(P(("ens", "gx"), "gy", None),) * 3 + (P("ens"),),
        check_vma=False,
    )
```

```python
import functools

import jax
import jax.numpy as jnp
from jax import lax
from jax.experimental import pallas as pl
from jax.experimental.pallas import tpu as pltpu
from jax.sharding import PartitionSpec as P

time_step = 0.2
head_slope = 0.5
molecular = 0.05
dispersivity = 0.1

RIM = 1
PAD = 8
DIRS = ((1, 0), (-1, 0), (0, 1), (0, -1), (1, 1), (1, -1), (-1, 1), (-1, -1))
MESH = pl.DeviceIdType.MESH


def split3(values):
    high = values.astype(jnp.bfloat16)
    rest = values - high.astype(jnp.float32)
    mid = rest.astype(jnp.bfloat16)
    low = (rest - mid.astype(jnp.float32)).astype(jnp.bfloat16)
    return high, mid, low


def dot_t(a, b):
    return lax.dot_general(a, b, (((1,), (1,)), ((), ())), preferred_element_type=jnp.float32)


def up_y(v):
    return pltpu.roll(v, v.shape[0] - 1, 0)


def down_y(v):
    return pltpu.roll(v, 1, 0)


def up_z(v):
    return pltpu.roll(v, v.shape[1] - 1, 1)


def down_z(v):
    return pltpu.roll(v, 1, 1)


def source_slices(dx, dy, lx, ly):
    width = RIM
    if dx == 0:
        xs, xd = (0, lx), RIM
    elif dx > 0:
        xs, xd = (lx - width, width), RIM - width
    else:
        xs, xd = (0, width), lx + RIM
    if dy == 0:
        ys, yd = (0, ly), PAD
    elif dy > 0:
        ys, yd = (ly - PAD, PAD), 0
    else:
        ys, yd = (0, PAD), ly + PAD
    return xs, ys, xd, yd


def out_plane(x, c0, c1, a1, a2, fu, fl, ky, kz, ly):
    v1, v2 = a1[x], a2[x]
    t0, t1 = c0[x], c1[x]
    lean = head_slope + dispersivity

    def face_x(p):
        low1 = lean * c1[p] - dispersivity * c1[p + 1]
        low0 = lean * c0[p] - dispersivity * c0[p + 1]
        d1 = a1[p + 1] - a1[p]
        d2 = a2[p + 1] - a2[p]
        return (fu[p] - fl[p]) * (d2 * low1 + d1 * low0), d1

    gx_up, above = face_x(x)
    gx_low, below = face_x(x - 1)
    grad = gx_up + gx_low
    new = v1 + (above * fu[x] - below * fl[x - 1])
    for k, up, down in ((ky[x], up_y, down_y), (kz[x], up_z, down_z)):
        d1 = up(v1) - v1
        flow = k * d1
        new = new + (flow - down(flow))
        sens = (d1 * (up(t0) - t0) + (up(v2) - v2) * (up(t1) - t1)) * (
            -0.5 * jnp.maximum(k - time_step * molecular, 0.0)
        )
        grad = grad + (sens + down(sens))
    return grad[PAD : PAD + ly], new[PAD : PAD + ly]


def finish(c0, c1, a1, a2, fu, fl, ky, kz, grad_in, adj_in, conc_in, grad, adj, conc, edge, sems):
    lx, ly, nz = conc.shape
    mid = pl.ds(1, lx - 2)
    copies = [
        pltpu.make_async_copy(conc_in, conc, sems.at[0]),
        pltpu.make_async_copy(grad_in.at[mid], grad.at[mid], sems.at[1]),
        pltpu.make_async_copy(adj_in.at[mid], adj.at[mid], sems.at[2]),
    ]
    for copy in copies:
        copy.start()
    for k, b in enumerate((0, lx - 1)):
        g, a = out_plane(b + RIM, c0, c1, a1, a2, fu, fl, ky, kz, ly)
        for slot, value, target in ((2 * k, g, grad), (2 * k + 1, a, adj)):
            edge[slot] = value
            copy = pltpu.make_async_copy(edge.at[slot], target.at[b], sems.at[3 + slot])
            copy.start()
            copies.append(copy)
    for copy in copies:
        copy.wait()


def kernel(
    nx,
    ny,
    lc_ref,
    c_ref,
    survey_ref,
    weight_ref,
    wcell_hbm,
    wdata_hbm,
    wweight_hbm,
    scell_hbm,
    srate_hbm,
    step_ref,
    c0,
    c1,
    a1,
    a2,
    fu,
    fl,
    ky,
    kz,
    grad_ref,
    adj_ref,
    conc_ref,
    misfit_ref,
    h,
    q,
    ww,
    wd,
    sv,
    sw,
    part,
    part_a,
    wcell_ref,
    wdata_ref,
    wweight_ref,
    scell_ref,
    srate_ref,
    red_y,
    red_x,
    local_sem,
    send1,
    recv1,
    send2,
    recv2,
    send_p,
    recv_p,
    send_y,
    recv_y,
    send_x,
    recv_x,
):
    f32 = jnp.float32
    lx, ly, nz = c_ref.shape
    rows = ly + 2 * PAD
    i = lax.axis_index("gx")
    j = lax.axis_index("gy")
    body = (slice(None), pl.ds(PAD, ly), slice(None))

    loads = [
        pltpu.make_async_copy(lc_ref, h.at[pl.ds(RIM, lx), pl.ds(PAD, ly)], local_sem.at[0]),
        pltpu.make_async_copy(c_ref, c0.at[pl.ds(RIM, lx), pl.ds(PAD, ly)], local_sem.at[1]),
        pltpu.make_async_copy(survey_ref, sv, local_sem.at[2]),
        pltpu.make_async_copy(weight_ref, sw, local_sem.at[3]),
    ]

    small = [
        pltpu.make_async_copy(src, dst, local_sem.at[4 + k])
        for k, (src, dst) in enumerate(
            (
                (wcell_hbm, wcell_ref),
                (wdata_hbm, wdata_ref),
                (wweight_hbm, wweight_ref),
                (scell_hbm, scell_ref),
                (srate_hbm, srate_ref),
            )
        )
    ]

    def inside(a, b):
        return (a >= 0) & (a < nx) & (b >= 0) & (b < ny)

    barrier = pltpu.get_barrier_semaphore()

    def greet(di, dj):
        pl.semaphore_signal(barrier, inc=1, device_id={"gx": di, "gy": dj}, device_id_type=MESH)

    for dx, dy in DIRS[4:]:

        @pl.when(inside(i + dx, j + dy))
        def _():
            greet(i + dx, j + dy)

    @pl.loop(1, nx)
    def _(o):
        greet(lax.rem(i + o, nx), j)

    @pl.loop(1, ny)
    def _(o):
        greet(i, lax.rem(j + o, ny))

    for load in small + loads:
        load.start()

    def one(flag):
        return jnp.where(flag, 1, 0)

    sides = (one(i > 0) + one(i < nx - 1)) * (one(j > 0) + one(j < ny - 1))
    pl.semaphore_wait(barrier, nx - 1 + ny - 1 + sides)

    def remote(d, src, dst, off_x, off_y, send, recv):
        dx, dy = DIRS[d]
        xs, ys, xd, yd = source_slices(dx, dy, lx, ly)
        return pltpu.make_async_remote_copy(
            src_ref=src.at[pl.ds(xs[0] + off_x, xs[1]), pl.ds(ys[0] + off_y, ys[1])],
            dst_ref=dst.at[pl.ds(xd, xs[1]), pl.ds(yd, ys[1])],
            send_sem=send,
            recv_sem=recv,
            device_id={"gx": i + dx, "gy": j + dy},
            device_id_type=MESH,
        )

    first = [
        [
            remote(d, c_ref, c0, 0, 0, send1.at[2 * d], recv1.at[2 * d]),
            remote(d, lc_ref, h, 0, 0, send1.at[2 * d + 1], recv1.at[2 * d + 1]),
        ]
        for d in range(8)
    ]
    second = [[remote(d, a2, a2, RIM, PAD, send2.at[d], recv2.at[d])] for d in range(8)]

    def partial_copy(k, src, dst):
        up = k % 2 == 0
        return pltpu.make_async_remote_copy(
            src_ref=src.at[k % 2],
            dst_ref=dst.at[0 if up else lx + RIM, pl.ds(PAD, ly)],
            send_sem=send_p.at[k],
            recv_sem=recv_p.at[k],
            device_id={"gx": i + 1 if up else i - 1, "gy": j},
            device_id_type=MESH,
        )

    third = [[partial_copy(k, part, c1)] for k in range(2)]
    fourth = [[partial_copy(2 + k, part_a, a1)] for k in range(2)]

    def start(copies, d):
        dx, dy = DIRS[d]

        @pl.when(inside(i + dx, j + dy))
        def _():
            for copy in copies[d]:
                copy.start()

    def arrive(copies, d):
        dx, dy = DIRS[d]

        @pl.when(inside(i - dx, j - dy))
        def _():
            for copy in copies[d]:
                copy.wait_recv()

    def sent(copies, d):
        dx, dy = DIRS[d]

        @pl.when(inside(i + dx, j + dy))
        def _():
            for copy in copies[d]:
                copy.wait_send()

    for d in (2, 3, 4, 5, 6, 7, 0, 1):
        start(first, d)

    def fill(d, refs):
        dx, dy = DIRS[d]
        xs, ys, xd, yd = source_slices(dx, dy, lx, ly)

        @pl.when(jnp.logical_not(inside(i - dx, j - dy)))
        def _():
            for ref in refs:
                ref[pl.ds(xd, xs[1]), pl.ds(yd, ys[1])] = jnp.zeros((xs[1], ys[1], nz), f32)

    for d in range(8):
        fill(d, (c0, h, a2) if d > 1 else (c0, h, a2, c1, a1))
    for ref in (c1, a1):
        for x in (0, lx + 2 * RIM - 1):
            for y in (0, ly + PAD):
                ref[x, pl.ds(y, PAD)] = jnp.zeros((PAD, nz), f32)

    for load in small:
        load.wait()
    grid_y = ly * ny
    wcell = wcell_ref[...].reshape(1, -1)
    scell = scell_ref[...].reshape(1, -1)
    wweight = wweight_ref[...].reshape(1, -1)
    wdata = wdata_ref[...].reshape(1, -1)
    srate = srate_ref[...].reshape(1, -1)
    nobs, nsrc = wcell.shape[1], scell.shape[1]
    zi = lax.broadcasted_iota(jnp.int32, (nz, nobs), 0)
    at_z = zi == lax.rem(wcell, nz)
    well_parts = []
    for part_w, part_d in zip(split3(wweight), split3(wweight * wdata)):
        both = [jnp.where(at_z, p.astype(f32), 0.0).astype(jnp.bfloat16) for p in (part_w, part_d)]
        well_parts.append(jnp.concatenate(both, axis=0))
    src_z = lax.broadcasted_iota(jnp.int32, (nz, nsrc), 0) == lax.rem(scell, nz)
    src_parts = [jnp.where(src_z, p.astype(f32), 0.0).astype(jnp.bfloat16) for p in split3(srate)]
    src_parts = jnp.concatenate(src_parts, axis=0)
    well_row = lax.div(wcell, nz) - (i * lx * grid_y + j * ly)
    src_row = lax.div(scell, nz) - (i * lx * grid_y + j * ly)
    well_iota = lax.broadcasted_iota(jnp.int32, (ly, nobs), 0)
    src_iota = lax.broadcasted_iota(jnp.int32, (rows, nsrc), 0) - PAD

    def place_wells(x):
        hot = jnp.where(well_iota == well_row - x * grid_y, 1.0, 0.0).astype(jnp.bfloat16)
        both = dot_t(hot, well_parts[0]) + dot_t(hot, well_parts[1]) + dot_t(hot, well_parts[2])
        ww[x] = both[:, :nz]
        wd[x] = both[:, nz:]

    def place_sources(x):
        hot = jnp.where(src_iota == src_row - x * grid_y, 1.0, 0.0).astype(jnp.bfloat16)
        parts = dot_t(hot, src_parts)
        q[x] = parts[:, :nz] + parts[:, nz : 2 * nz] + parts[:, 2 * nz :]

    clock = jnp.full((1, nz), step_ref[0], jnp.int32).astype(f32)
    gain_first = time_step * (1.0 + 0.5 * jnp.sin(0.05 * clock))
    gain_second = time_step * (1.0 + 0.5 * jnp.sin(0.05 * (clock + 1.0)))

    lane = lax.broadcasted_iota(jnp.int32, (rows, nz), 1)
    row = lax.broadcasted_iota(jnp.int32, (rows, nz), 0)
    low_face = jnp.where(j == 0, PAD - 1, -1)
    high_face = jnp.where(j == ny - 1, PAD + ly - 1, -1)

    def faces_in(x):
        open_z = lane < nz - 1
        open_y = (row != low_face) & (row != high_face)
        half = h[x]
        ky[x] = jnp.where(
            open_y, time_step * molecular + time_step * dispersivity * (half * up_y(half)), 0.0
        )
        kz[x] = jnp.where(
            open_z, time_step * molecular + time_step * dispersivity * (half * up_z(half)), 0.0
        )

    def root(x):
        h[x] = jnp.exp(0.5 * h[x])

    def faces_x(x):
        cond = time_step * (h[x] * h[x + 1])
        closed = ((i == 0) & (x == RIM - 1)) | ((i == nx - 1) & (x == RIM + lx - 1))
        keep = jnp.where(closed, 0.0, 1.0)
        fu[x] = keep * (time_step * molecular + (head_slope + dispersivity) * cond)
        fl[x] = keep * (time_step * molecular + dispersivity * cond)

    def spread_yz(v, x):
        gy = ky[x] * (up_y(v) - v)
        gz = kz[x] * (up_z(v) - v)
        return (gy - down_y(gy)) + (gz - down_z(gz))

    def forward(src, x):
        v = src[x]
        out = fu[x] * v - fl[x] * src[x + 1]
        into = fu[x - 1] * src[x - 1] - fl[x - 1] * v
        return v + ((into - out) + spread_yz(v, x))

    def backward(src, x):
        v = src[x]
        above = src[x + 1] - v
        below = v - src[x - 1]
        return v + ((above * fu[x] - below * fl[x - 1]) + spread_yz(v, x))

    def do_c1(x):
        c1[x] = forward(c0, x) + gain_first * q[x - RIM]

    def do_c2(x, total):
        final = (forward(c1, x) + gain_second * q[x - RIM])[PAD : PAD + ly]
        b = x - RIM
        conc_ref[b] = final
        missed = final - sv[b]
        seed = sw[b] * missed
        heavy = ww[b] * final
        pulled = wd[b]
        a2[x, pl.ds(PAD, ly)] = seed + (heavy - pulled)
        term = seed * missed + final * (heavy - 2.0 * pulled)
        return total + jnp.sum(term.reshape(ly // 8, 8, nz), axis=0)

    def do_a1(x):
        a1[x] = backward(a2, x)

    def do_out(x):
        g, a = out_plane(x, c0, c1, a1, a2, fu, fl, ky, kz, ly)
        grad_ref[x - RIM] = g
        adj_ref[x - RIM] = a

    def loop(low, high, f):
        @pl.loop(low, high)
        def _(x):
            f(x)

    lo, hi = RIM, RIM + lx
    for load in loads:
        load.wait()
    place_sources(0)
    place_sources(lx - 1)
    for d in (2, 3):
        arrive(first, d)
    for x in (lo, lo + 1, hi - 2, hi - 1):
        root(x)
    for x in (lo, hi - 1):
        faces_in(x)
    faces_x(lo)
    faces_x(hi - 2)
    v = c0[hi - 1]
    top = v + (fu[hi - 2] * c0[hi - 2] - fl[hi - 2] * v) + spread_yz(v, hi - 1)
    c1[hi - 1] = top + gain_first * q[lx - 1]
    part[0] = c1[hi - 1, pl.ds(PAD, ly)]
    v = c0[lo]
    bottom = v - (fu[lo] * v - fl[lo] * c0[lo + 1]) + spread_yz(v, lo)
    c1[lo] = bottom + gain_first * q[0]
    part[1] = c1[lo, pl.ds(PAD, ly)]
    start(third, 0)
    start(third, 1)

    loop(1, lx - 1, place_sources)
    loop(lo + 2, hi - 2, root)
    loop(lo + 1, hi - 1, faces_in)
    loop(lo + 1, hi - 2, faces_x)
    loop(lo + 1, hi - 1, do_c1)
    loop(0, lx, place_wells)
    total = lax.fori_loop(lo + 2, hi - 2, do_c2, jnp.zeros((8, nz), f32))

    for d in (0, 1, 4, 5, 6, 7):
        arrive(first, d)
    root(lo - 1)
    root(hi)
    faces_x(lo - 1)
    faces_x(hi - 1)
    flux_low = fu[lo - 1] * c0[lo - 1] - fl[lo - 1] * c0[lo]
    flux_high = fu[hi - 1] * c0[hi - 1] - fl[hi - 1] * c0[hi]
    c1[lo] = c1[lo] + flux_low
    c1[hi - 1] = c1[hi - 1] - flux_high
    total = do_c2(lo + 1, total)
    total = do_c2(hi - 2, total)
    arrive(third, 0)
    arrive(third, 1)
    c1[lo - 1] = c1[lo - 1] - flux_low
    c1[hi] = c1[hi] + flux_high
    total = do_c2(lo, total)
    total = do_c2(hi - 1, total)

    def reduce_start(ref, axis, me, count, send, recv):
        @pl.loop(1, count)
        def _(o):
            pltpu.make_async_remote_copy(
                src_ref=ref.at[me],
                dst_ref=ref.at[me],
                send_sem=send.at[o],
                recv_sem=recv.at[me],
                device_id={axis: lax.rem(me + o, count)},
                device_id_type=MESH,
            ).start()

    def reduce_wait(ref, axis, me, count, send, recv):
        @pl.loop(1, count)
        def _(o):
            other = lax.rem(me + o, count)
            copy = pltpu.make_async_remote_copy(
                src_ref=ref.at[me],
                dst_ref=ref.at[other],
                send_sem=send.at[o],
                recv_sem=recv.at[other],
                device_id={axis: other},
                device_id_type=MESH,
            )
            copy.wait_send()
            copy.wait_recv()

    red_x[i] = total
    reduce_start(red_x, "gx", i, nx, send_x, recv_x)
    for d in (2, 3, 4, 5, 6, 7, 0, 1):
        start(second, d)

    for d in (2, 3):
        arrive(second, d)
    v = a2[hi - 1]
    a1[hi - 1] = v - (v - a2[hi - 2]) * fl[hi - 2] + spread_yz(v, hi - 1)
    part_a[0] = a1[hi - 1, pl.ds(PAD, ly)]
    v = a2[lo]
    a1[lo] = v + (a2[lo + 1] - v) * fu[lo] + spread_yz(v, lo)
    part_a[1] = a1[lo, pl.ds(PAD, ly)]
    start(fourth, 0)
    start(fourth, 1)

    loop(lo + 1, hi - 1, do_a1)
    reduce_wait(red_x, "gx", i, nx, send_x, recv_x)
    red_y[j] = jnp.sum(red_x[...], axis=0)
    reduce_start(red_y, "gy", j, ny, send_y, recv_y)

    for d in (0, 1, 4, 5, 6, 7):
        arrive(second, d)
    gap_low = a2[lo] - a2[lo - 1]
    gap_high = a2[hi] - a2[hi - 1]
    a1[lo] = a1[lo] - gap_low * fl[lo - 1]
    a1[hi - 1] = a1[hi - 1] + gap_high * fu[hi - 1]
    loop(lo + 1, hi - 1, do_out)
    arrive(fourth, 0)
    arrive(fourth, 1)
    a1[lo - 1] = a1[lo - 1] + gap_low * fu[lo - 1]
    a1[hi] = a1[hi] - gap_high * fl[hi - 1]

    reduce_wait(red_y, "gy", j, ny, send_y, recv_y)
    wells = jnp.sum(wweight * wdata * wdata)
    whole = jnp.sum(jnp.sum(red_y[...], axis=0)) + wells
    misfit_ref[0] = whole * (0.5 / (nx * lx * grid_y * nz))
    for d in range(8):
        sent(first, d)
        sent(second, d)
    for k in range(2):
        sent(third, k)
        sent(fourth, k)


def on_device(*args):
    lx, ly, nz = args[1].shape
    nx = lax.axis_size("gx")
    ny = lax.axis_size("gy")
    rows = ly + 2 * PAD
    wide = (lx + 2 * RIM, rows, nz)
    block = (lx, ly, nz)
    hbm = pl.BlockSpec(memory_space=pltpu.HBM)
    vmem = pl.BlockSpec(memory_space=pltpu.VMEM)
    smem = pl.BlockSpec(memory_space=pltpu.SMEM)
    dma = pltpu.SemaphoreType.DMA
    f32 = jnp.float32
    pinned = [pltpu.with_memory_space_constraint(a, pltpu.HBM) for a in args[:9]]
    *fields, misfit = pl.pallas_call(
        functools.partial(kernel, nx, ny),
        out_shape=[pltpu.VMEM(wide, f32)] * 8
        + [pltpu.VMEM(block, f32)] * 3
        + [jax.ShapeDtypeStruct((1,), f32)],
        in_specs=[hbm] * 9 + [smem],
        out_specs=[vmem] * 11 + [smem],
        scratch_shapes=[pltpu.VMEM(wide, f32), pltpu.VMEM((lx, rows, nz), f32)]
        + [pltpu.VMEM(block, f32)] * 4
        + [pltpu.VMEM((2, ly, nz), f32)] * 2
        + [pltpu.VMEM(a.shape, a.dtype) for a in args[4:9]]
        + [pltpu.VMEM((ny, 8, nz), f32), pltpu.VMEM((nx, 8, nz), f32)]
        + [dma((9,)), dma((16,)), dma((16,)), dma((8,)), dma((8,)), dma((4,)), dma((4,))]
        + [dma((ny,)), dma((ny,)), dma((nx,)), dma((nx,))],
        compiler_params=pltpu.CompilerParams(
            collective_id=0, has_side_effects=True, vmem_limit_bytes=24 * 1024 * 1024
        ),
    )(*pinned, args[9])
    grad, adj, conc = pl.pallas_call(
        finish,
        out_shape=[pltpu.HBM(block, f32)] * 3,
        in_specs=[vmem] * 11,
        out_specs=[hbm] * 3,
        scratch_shapes=[pltpu.VMEM((4, ly, nz), f32), dma((7,))],
        compiler_params=pltpu.CompilerParams(vmem_limit_bytes=24 * 1024 * 1024),
    )(*fields)
    return grad, adj, conc, misfit


def solution(mesh):
    return jax.shard_map(
        on_device,
        mesh=mesh,
        in_specs=(P(("ens", "gx"), "gy", None),) * 4 + (P("ens"),) * 6,
        out_specs=(P(("ens", "gx"), "gy", None),) * 3 + (P("ens"),),
        check_vma=False,
    )
```

```python
import functools

import jax
import jax.numpy as jnp
from jax import lax
from jax.experimental import pallas as pl
from jax.experimental.pallas import tpu as pltpu
from jax.sharding import PartitionSpec as P

time_step = 0.2
head_slope = 0.5
molecular = 0.05
dispersivity = 0.1

RIM = 1
PAD = 8
DIRS = ((1, 0), (-1, 0), (0, 1), (0, -1), (1, 1), (1, -1), (-1, 1), (-1, -1))
MESH = pl.DeviceIdType.MESH


def split3(values):
    high = values.astype(jnp.bfloat16)
    rest = values - high.astype(jnp.float32)
    mid = rest.astype(jnp.bfloat16)
    low = (rest - mid.astype(jnp.float32)).astype(jnp.bfloat16)
    return high, mid, low


def dot_t(a, b):
    return lax.dot_general(a, b, (((1,), (1,)), ((), ())), preferred_element_type=jnp.float32)


def up_y(v):
    return pltpu.roll(v, v.shape[0] - 1, 0)


def down_y(v):
    return pltpu.roll(v, 1, 0)


def up_z(v):
    return pltpu.roll(v, v.shape[1] - 1, 1)


def down_z(v):
    return pltpu.roll(v, 1, 1)


def source_slices(dx, dy, lx, ly):
    width = RIM
    if dx == 0:
        xs, xd = (0, lx), RIM
    elif dx > 0:
        xs, xd = (lx - width, width), RIM - width
    else:
        xs, xd = (0, width), lx + RIM
    if dy == 0:
        ys, yd = (0, ly), PAD
    elif dy > 0:
        ys, yd = (ly - 2, 2), PAD - 2
    else:
        ys, yd = (0, 2), ly + PAD
    return xs, ys, xd, yd


def out_plane(x, c0, c1, a1, a2, fu, fl, ky, kz, ly):
    v1, v2 = a1[x], a2[x]
    t0, t1 = c0[x], c1[x]
    lean = head_slope + dispersivity

    def face_x(p):
        low1 = lean * c1[p] - dispersivity * c1[p + 1]
        low0 = lean * c0[p] - dispersivity * c0[p + 1]
        d1 = a1[p + 1] - a1[p]
        d2 = a2[p + 1] - a2[p]
        return (fu[p] - fl[p]) * (d2 * low1 + d1 * low0), d1

    gx_up, above = face_x(x)
    gx_low, below = face_x(x - 1)
    grad = gx_up + gx_low
    new = v1 + (above * fu[x] - below * fl[x - 1])
    for k, up, down in ((ky[x], up_y, down_y), (kz[x], up_z, down_z)):
        d1 = up(v1) - v1
        flow = k * d1
        new = new + (flow - down(flow))
        sens = (d1 * (up(t0) - t0) + (up(v2) - v2) * (up(t1) - t1)) * (
            -0.5 * jnp.maximum(k - time_step * molecular, 0.0)
        )
        grad = grad + (sens + down(sens))
    return grad[PAD : PAD + ly], new[PAD : PAD + ly]


def finish(c0, c1, a1, a2, fu, fl, ky, kz, grad_in, adj_in, conc_in, grad, adj, conc, edge, sems):
    lx, ly, nz = conc.shape
    mid = pl.ds(1, lx - 2)
    copies = [
        pltpu.make_async_copy(conc_in, conc, sems.at[0]),
        pltpu.make_async_copy(grad_in.at[mid], grad.at[mid], sems.at[1]),
        pltpu.make_async_copy(adj_in.at[mid], adj.at[mid], sems.at[2]),
    ]
    for copy in copies:
        copy.start()
    for k, b in enumerate((0, lx - 1)):
        g, a = out_plane(b + RIM, c0, c1, a1, a2, fu, fl, ky, kz, ly)
        for slot, value, target in ((2 * k, g, grad), (2 * k + 1, a, adj)):
            edge[slot] = value
            copy = pltpu.make_async_copy(edge.at[slot], target.at[b], sems.at[3 + slot])
            copy.start()
            copies.append(copy)
    for copy in copies:
        copy.wait()


def kernel(
    nx,
    ny,
    lc_ref,
    c_ref,
    survey_ref,
    weight_ref,
    wcell_hbm,
    wdata_hbm,
    wweight_hbm,
    scell_hbm,
    srate_hbm,
    step_ref,
    c0,
    c1,
    a1,
    a2,
    fu,
    fl,
    ky,
    kz,
    grad_ref,
    adj_ref,
    conc_ref,
    misfit_ref,
    h,
    q,
    ww,
    wd,
    sv,
    sw,
    part,
    part_a,
    wcell_ref,
    wdata_ref,
    wweight_ref,
    scell_ref,
    srate_ref,
    red_y,
    red_x,
    local_sem,
    send1,
    recv1,
    send2,
    recv2,
    send_p,
    recv_p,
    send_y,
    recv_y,
    send_x,
    recv_x,
):
    f32 = jnp.float32
    lx, ly, nz = c_ref.shape
    rows = ly + 2 * PAD
    i = lax.axis_index("gx")
    j = lax.axis_index("gy")
    body = (slice(None), pl.ds(PAD, ly), slice(None))

    loads = [
        pltpu.make_async_copy(lc_ref, h.at[pl.ds(RIM, lx), pl.ds(PAD, ly)], local_sem.at[0]),
        pltpu.make_async_copy(c_ref, c0.at[pl.ds(RIM, lx), pl.ds(PAD, ly)], local_sem.at[1]),
        pltpu.make_async_copy(survey_ref, sv, local_sem.at[2]),
        pltpu.make_async_copy(weight_ref, sw, local_sem.at[3]),
    ]

    small = [
        pltpu.make_async_copy(src, dst, local_sem.at[4 + k])
        for k, (src, dst) in enumerate(
            (
                (wcell_hbm, wcell_ref),
                (wdata_hbm, wdata_ref),
                (wweight_hbm, wweight_ref),
                (scell_hbm, scell_ref),
                (srate_hbm, srate_ref),
            )
        )
    ]

    def inside(a, b):
        return (a >= 0) & (a < nx) & (b >= 0) & (b < ny)

    barrier = pltpu.get_barrier_semaphore()

    def greet(di, dj):
        pl.semaphore_signal(barrier, inc=1, device_id={"gx": di, "gy": dj}, device_id_type=MESH)

    for dx, dy in DIRS[4:]:

        @pl.when(inside(i + dx, j + dy))
        def _():
            greet(i + dx, j + dy)

    @pl.loop(1, nx)
    def _(o):
        greet(lax.rem(i + o, nx), j)

    @pl.loop(1, ny)
    def _(o):
        greet(i, lax.rem(j + o, ny))

    for load in small + loads:
        load.start()

    grid_y = ly * ny
    origin = i * lx * grid_y + j * ly

    def hot_rows(cells, count, pad):
        shape = (lx, count, cells.shape[1])
        line = lax.broadcasted_iota(jnp.int32, shape, 0) * grid_y + (
            lax.broadcasted_iota(jnp.int32, shape, 1) - pad
        )
        target = lax.div(cells, nz) - origin
        hot = jnp.where(line == target.reshape(1, 1, -1), 1.0, 0.0)
        return hot.reshape(lx * count, -1).astype(jnp.bfloat16)

    def hot_lanes(cells, values):
        shape = (nz, cells.shape[1])
        at_z = lax.broadcasted_iota(jnp.int32, shape, 0) == lax.rem(cells, nz)
        return [jnp.where(at_z, p.astype(f32), 0.0).astype(jnp.bfloat16) for p in split3(values)]

    def place_sources():
        scell = scell_ref[...].reshape(1, -1)
        srate = srate_ref[...].reshape(1, -1)
        weights = jnp.concatenate(hot_lanes(scell, srate), axis=0)
        parts = dot_t(hot_rows(scell, rows, PAD), weights)
        both = parts[:, :nz] + parts[:, nz : 2 * nz] + parts[:, 2 * nz :]
        q[...] = both.reshape(lx, rows, nz)

    def place_wells():
        wcell = wcell_ref[...].reshape(1, -1)
        wweight = wweight_ref[...].reshape(1, -1)
        wdata = wdata_ref[...].reshape(1, -1)
        hot = hot_rows(wcell, ly, 0)
        for target, values in ((ww, wweight), (wd, wweight * wdata)):
            weights = jnp.concatenate(hot_lanes(wcell, values), axis=0)
            parts = dot_t(hot, weights)
            both = parts[:, :nz] + parts[:, nz : 2 * nz] + parts[:, 2 * nz :]
            target[...] = both.reshape(lx, ly, nz)
        return jnp.sum(wweight * wdata * wdata)

    for load in small:
        load.wait()
    place_sources()

    def one(flag):
        return jnp.where(flag, 1, 0)

    sides = (one(i > 0) + one(i < nx - 1)) * (one(j > 0) + one(j < ny - 1))
    pl.semaphore_wait(barrier, nx - 1 + ny - 1 + sides)

    def remote(d, src, dst, off_x, off_y, send, recv):
        dx, dy = DIRS[d]
        xs, ys, xd, yd = source_slices(dx, dy, lx, ly)
        return pltpu.make_async_remote_copy(
            src_ref=src.at[pl.ds(xs[0] + off_x, xs[1]), pl.ds(ys[0] + off_y, ys[1])],
            dst_ref=dst.at[pl.ds(xd, xs[1]), pl.ds(yd, ys[1])],
            send_sem=send,
            recv_sem=recv,
            device_id={"gx": i + dx, "gy": j + dy},
            device_id_type=MESH,
        )

    first = [
        [
            remote(d, c_ref, c0, 0, 0, send1.at[2 * d], recv1.at[2 * d]),
            remote(d, lc_ref, h, 0, 0, send1.at[2 * d + 1], recv1.at[2 * d + 1]),
        ]
        for d in range(8)
    ]
    second = [[remote(d, a2, a2, RIM, PAD, send2.at[d], recv2.at[d])] for d in range(8)]

    def partial_copy(k, src, dst):
        up = k % 2 == 0
        return pltpu.make_async_remote_copy(
            src_ref=src.at[k % 2],
            dst_ref=dst.at[0 if up else lx + RIM, pl.ds(PAD, ly)],
            send_sem=send_p.at[k],
            recv_sem=recv_p.at[k],
            device_id={"gx": i + 1 if up else i - 1, "gy": j},
            device_id_type=MESH,
        )

    third = [[partial_copy(k, part, c1)] for k in range(2)]
    fourth = [[partial_copy(2 + k, part_a, a1)] for k in range(2)]

    def start(copies, d):
        dx, dy = DIRS[d]

        @pl.when(inside(i + dx, j + dy))
        def _():
            for copy in copies[d]:
                copy.start()

    def arrive(copies, d):
        dx, dy = DIRS[d]

        @pl.when(inside(i - dx, j - dy))
        def _():
            for copy in copies[d]:
                copy.wait_recv()

    def sent(copies, d):
        dx, dy = DIRS[d]

        @pl.when(inside(i + dx, j + dy))
        def _():
            for copy in copies[d]:
                copy.wait_send()

    for d in (2, 3, 4, 5, 6, 7, 0, 1):
        start(first, d)

    def fill(d, refs):
        dx, dy = DIRS[d]
        xs, ys, xd, yd = source_slices(dx, dy, lx, ly)

        @pl.when(jnp.logical_not(inside(i - dx, j - dy)))
        def _():
            for ref in refs:
                ref[pl.ds(xd, xs[1]), pl.ds(yd, ys[1])] = jnp.zeros((xs[1], ys[1], nz), f32)

    for d in range(8):
        fill(d, (c0, h, a2) if d > 1 else (c0, h, a2, c1, a1))
    for ref in (c1, a1):
        for x in (0, lx + 2 * RIM - 1):
            for y in (0, ly + PAD):
                ref[x, pl.ds(y, PAD)] = jnp.zeros((PAD, nz), f32)

    clock = jnp.full((1, nz), step_ref[0], jnp.int32).astype(f32)
    gain_first = time_step * (1.0 + 0.5 * jnp.sin(0.05 * clock))
    gain_second = time_step * (1.0 + 0.5 * jnp.sin(0.05 * (clock + 1.0)))

    lane = lax.broadcasted_iota(jnp.int32, (rows, nz), 1)
    row = lax.broadcasted_iota(jnp.int32, (rows, nz), 0)
    low_face = jnp.where(j == 0, PAD - 1, -1)
    high_face = jnp.where(j == ny - 1, PAD + ly - 1, -1)

    def faces_in(x):
        open_z = lane < nz - 1
        open_y = (row != low_face) & (row != high_face)
        half = h[x]
        ky[x] = jnp.where(
            open_y, time_step * molecular + time_step * dispersivity * (half * up_y(half)), 0.0
        )
        kz[x] = jnp.where(
            open_z, time_step * molecular + time_step * dispersivity * (half * up_z(half)), 0.0
        )

    def root(x):
        h[x] = jnp.exp(0.5 * h[x])

    def faces_x(x):
        cond = time_step * (h[x] * h[x + 1])
        closed = ((i == 0) & (x == RIM - 1)) | ((i == nx - 1) & (x == RIM + lx - 1))
        keep = jnp.where(closed, 0.0, 1.0)
        fu[x] = keep * (time_step * molecular + (head_slope + dispersivity) * cond)
        fl[x] = keep * (time_step * molecular + dispersivity * cond)

    def spread_yz(v, x):
        gy = ky[x] * (up_y(v) - v)
        gz = kz[x] * (up_z(v) - v)
        return (gy - down_y(gy)) + (gz - down_z(gz))

    def forward(src, x):
        v = src[x]
        out = fu[x] * v - fl[x] * src[x + 1]
        into = fu[x - 1] * src[x - 1] - fl[x - 1] * v
        return v + ((into - out) + spread_yz(v, x))

    def backward(src, x):
        v = src[x]
        above = src[x + 1] - v
        below = v - src[x - 1]
        return v + ((above * fu[x] - below * fl[x - 1]) + spread_yz(v, x))

    def do_c1(x):
        c1[x] = forward(c0, x) + gain_first * q[x - RIM]

    def do_c2(x, total):
        final = (forward(c1, x) + gain_second * q[x - RIM])[PAD : PAD + ly]
        b = x - RIM
        conc_ref[b] = final
        missed = final - sv[b]
        seed = sw[b] * missed
        heavy = ww[b] * final
        pulled = wd[b]
        a2[x, pl.ds(PAD, ly)] = seed + (heavy - pulled)
        term = seed * missed + final * (heavy - 2.0 * pulled)
        return total + jnp.sum(term.reshape(ly // 8, 8, nz), axis=0)

    def do_a1(x):
        a1[x] = backward(a2, x)

    def do_out(x):
        g, a = out_plane(x, c0, c1, a1, a2, fu, fl, ky, kz, ly)
        grad_ref[x - RIM] = g
        adj_ref[x - RIM] = a

    def loop(low, high, f):
        @pl.loop(low, high)
        def _(x):
            f(x)

    lo, hi = RIM, RIM + lx
    wells = place_wells()
    for load in loads:
        load.wait()

    @pl.loop(lo, hi)
    def _(x):
        h[x, pl.ds(PAD, ly)] = jnp.exp(0.5 * h[x, pl.ds(PAD, ly)])

    for d in (2, 3):
        arrive(first, d)

    @pl.loop(lo, hi)
    def _(x):
        for y in (0, PAD + ly):
            h[x, pl.ds(y, PAD)] = jnp.exp(0.5 * h[x, pl.ds(y, PAD)])

    for x in (lo, hi - 1):
        faces_in(x)
    faces_x(lo)
    faces_x(hi - 2)
    v = c0[hi - 1]
    top = v + (fu[hi - 2] * c0[hi - 2] - fl[hi - 2] * v) + spread_yz(v, hi - 1)
    c1[hi - 1] = top + gain_first * q[lx - 1]
    part[0] = c1[hi - 1, pl.ds(PAD, ly)]
    v = c0[lo]
    bottom = v - (fu[lo] * v - fl[lo] * c0[lo + 1]) + spread_yz(v, lo)
    c1[lo] = bottom + gain_first * q[0]
    part[1] = c1[lo, pl.ds(PAD, ly)]
    start(third, 0)
    start(third, 1)

    loop(lo + 1, hi - 1, faces_in)
    loop(lo + 1, hi - 2, faces_x)
    loop(lo + 1, hi - 1, do_c1)
    total = lax.fori_loop(lo + 2, hi - 2, do_c2, jnp.zeros((8, nz), f32))

    for d in (0, 1, 4, 5, 6, 7):
        arrive(first, d)
    root(lo - 1)
    root(hi)
    faces_x(lo - 1)
    faces_x(hi - 1)
    flux_low = fu[lo - 1] * c0[lo - 1] - fl[lo - 1] * c0[lo]
    flux_high = fu[hi - 1] * c0[hi - 1] - fl[hi - 1] * c0[hi]
    c1[lo] = c1[lo] + flux_low
    c1[hi - 1] = c1[hi - 1] - flux_high
    total = do_c2(lo + 1, total)
    total = do_c2(hi - 2, total)
    arrive(third, 0)
    arrive(third, 1)
    c1[lo - 1] = c1[lo - 1] - flux_low
    c1[hi] = c1[hi] + flux_high
    total = do_c2(lo, total)
    total = do_c2(hi - 1, total)

    def reduce_start(ref, axis, me, count, send, recv):
        @pl.loop(1, count)
        def _(o):
            pltpu.make_async_remote_copy(
                src_ref=ref.at[me],
                dst_ref=ref.at[me],
                send_sem=send.at[o],
                recv_sem=recv.at[me],
                device_id={axis: lax.rem(me + o, count)},
                device_id_type=MESH,
            ).start()

    def reduce_wait(ref, axis, me, count, send, recv):
        @pl.loop(1, count)
        def _(o):
            other = lax.rem(me + o, count)
            copy = pltpu.make_async_remote_copy(
                src_ref=ref.at[me],
                dst_ref=ref.at[other],
                send_sem=send.at[o],
                recv_sem=recv.at[other],
                device_id={axis: other},
                device_id_type=MESH,
            )
            copy.wait_send()
            copy.wait_recv()

    red_x[i] = total
    reduce_start(red_x, "gx", i, nx, send_x, recv_x)
    for d in (2, 3, 4, 5, 6, 7, 0, 1):
        start(second, d)

    for d in (2, 3):
        arrive(second, d)
    v = a2[hi - 1]
    a1[hi - 1] = v - (v - a2[hi - 2]) * fl[hi - 2] + spread_yz(v, hi - 1)
    part_a[0] = a1[hi - 1, pl.ds(PAD, ly)]
    v = a2[lo]
    a1[lo] = v + (a2[lo + 1] - v) * fu[lo] + spread_yz(v, lo)
    part_a[1] = a1[lo, pl.ds(PAD, ly)]
    start(fourth, 0)
    start(fourth, 1)

    loop(lo + 1, hi - 1, do_a1)
    reduce_wait(red_x, "gx", i, nx, send_x, recv_x)
    red_y[j] = jnp.sum(red_x[...], axis=0)
    reduce_start(red_y, "gy", j, ny, send_y, recv_y)

    for d in (0, 1, 4, 5, 6, 7):
        arrive(second, d)
    gap_low = a2[lo] - a2[lo - 1]
    gap_high = a2[hi] - a2[hi - 1]
    a1[lo] = a1[lo] - gap_low * fl[lo - 1]
    a1[hi - 1] = a1[hi - 1] + gap_high * fu[hi - 1]
    loop(lo + 1, hi - 1, do_out)
    arrive(fourth, 0)
    arrive(fourth, 1)
    a1[lo - 1] = a1[lo - 1] + gap_low * fu[lo - 1]
    a1[hi] = a1[hi] - gap_high * fl[hi - 1]

    reduce_wait(red_y, "gy", j, ny, send_y, recv_y)
    whole = jnp.sum(jnp.sum(red_y[...], axis=0)) + wells
    misfit_ref[0] = whole * (0.5 / (nx * lx * grid_y * nz))
    for d in range(8):
        sent(first, d)
        sent(second, d)
    for k in range(2):
        sent(third, k)
        sent(fourth, k)


def on_device(*args):
    lx, ly, nz = args[1].shape
    nx = lax.axis_size("gx")
    ny = lax.axis_size("gy")
    rows = ly + 2 * PAD
    wide = (lx + 2 * RIM, rows, nz)
    block = (lx, ly, nz)
    hbm = pl.BlockSpec(memory_space=pltpu.HBM)
    vmem = pl.BlockSpec(memory_space=pltpu.VMEM)
    smem = pl.BlockSpec(memory_space=pltpu.SMEM)
    dma = pltpu.SemaphoreType.DMA
    f32 = jnp.float32
    pinned = [pltpu.with_memory_space_constraint(a, pltpu.HBM) for a in args[:9]]
    *fields, misfit = pl.pallas_call(
        functools.partial(kernel, nx, ny),
        out_shape=[pltpu.VMEM(wide, f32)] * 8
        + [pltpu.VMEM(block, f32)] * 3
        + [jax.ShapeDtypeStruct((1,), f32)],
        in_specs=[hbm] * 9 + [smem],
        out_specs=[vmem] * 11 + [smem],
        scratch_shapes=[pltpu.VMEM(wide, f32), pltpu.VMEM((lx, rows, nz), f32)]
        + [pltpu.VMEM(block, f32)] * 4
        + [pltpu.VMEM((2, ly, nz), f32)] * 2
        + [pltpu.VMEM(a.shape, a.dtype) for a in args[4:9]]
        + [pltpu.VMEM((ny, 8, nz), f32), pltpu.VMEM((nx, 8, nz), f32)]
        + [dma((9,)), dma((16,)), dma((16,)), dma((8,)), dma((8,)), dma((4,)), dma((4,))]
        + [dma((ny,)), dma((ny,)), dma((nx,)), dma((nx,))],
        compiler_params=pltpu.CompilerParams(
            collective_id=0, has_side_effects=True, vmem_limit_bytes=24 * 1024 * 1024
        ),
    )(*pinned, args[9])
    grad, adj, conc = pl.pallas_call(
        finish,
        out_shape=[pltpu.HBM(block, f32)] * 3,
        in_specs=[vmem] * 11,
        out_specs=[hbm] * 3,
        scratch_shapes=[pltpu.VMEM((4, ly, nz), f32), dma((7,))],
        compiler_params=pltpu.CompilerParams(vmem_limit_bytes=24 * 1024 * 1024),
    )(*fields)
    return grad, adj, conc, misfit


def solution(mesh):
    return jax.shard_map(
        on_device,
        mesh=mesh,
        in_specs=(P(("ens", "gx"), "gy", None),) * 4 + (P("ens"),) * 6,
        out_specs=(P(("ens", "gx"), "gy", None),) * 3 + (P("ens"),),
        check_vma=False,
    )
```
